256 devices in a mesh: ctx: 128 (over x, y, z), kv: 2 (over core).
Axes of the slice: x: 4, y: 4, z: 8, core: 2. Of those that a mesh axis runs over, the one named last changes fastest.
Arguments:
- query_raw: bfloat16 [16384, 32, 128], P('ctx', 'kv')
- key_raw: bfloat16 [16384, 16, 128], P('ctx', 'kv')
- value_matrix: bfloat16 [16384, 16, 128], P('ctx', 'kv'), may hold values from -6 to 6
- query_gain: float32 [128], replicated, may hold values from 0.5 to 6
- key_gain: float32 [128], replicated, may hold values from 0.5 to 6
- doc_ids: int32 [16384], replicated, may hold values from 0 to 63, never falling along the last dimension, each value on 1 to 2048 neighbouring positions
- output_gradient: bfloat16 [16384, 32, 128], P('ctx', 'kv')
Outputs:
- query_grad: bfloat16 [16384, 32, 128], P('ctx', 'kv')
- key_grad: bfloat16 [16384, 16, 128], P('ctx', 'kv')
- value_grad: bfloat16 [16384, 16, 128], P('ctx', 'kv')
- query_gain_grad: float32 [128], replicated
- key_gain_grad: float32 [128], replicated
The draws below stay inside these ranges and needn't reach their ends.
Inputs may be any that keep to these rules, and one draw needn't show every extreme that they name: `doc_ids`: file numbers never fall along the sequence; every file has 1 to 2048 tokens and one has exactly 2048.
All inputs are finite; a program needn't handle non-finite values.
Results may differ from the reference program's by a relative error of at most 0.035.
The reference program's roundings to bfloat16 on the way count: a program that leaves them out, or rounds other values in their place, can miss the bound.
Values may be sent and summed in bfloat16 or wider, within the bound.
No kernel may reach another device: no remote copies, remote signals or barrier semaphores. Data moves between devices by JAX's collectives and lax.ppermute only.
A program may use at most 128 MiB of HBM per device.

```python
import math
import jax
import jax.numpy as jnp
import numpy as np
from jax import lax

QUERY_HEADS = 32
KEY_VALUE_HEADS = 16
HEAD_SIZE = 128
LOOKBACK_SPAN = 1024
TOKENS_PER_SHARD = 128
PACKED_TOKENS = 16384
N_CTX = 128


def raw_pair(key):
    fragments = jax.random.split(jax.random.fold_in(key, 7), 6)
    tenfold_group = math.log(10.0)
    row_query = jnp.exp(jax.random.uniform(fragments[0], (PACKED_TOKENS, QUERY_HEADS, 1), jnp.float32, 0.0, tenfold_group))
    row_key_part = jnp.exp(jax.random.uniform(fragments[1], (PACKED_TOKENS, KEY_VALUE_HEADS, 1), jnp.float32, 0.0, tenfold_group))
    col_query = jnp.exp(jax.random.uniform(fragments[2], (HEAD_SIZE,), jnp.float32, 0.0, tenfold_group))
    column_key_part = jnp.exp(jax.random.uniform(fragments[3], (HEAD_SIZE,), jnp.float32, 0.0, tenfold_group))
    query_dir = jax.random.truncated_normal(fragments[4], -4.0, 4.0, (PACKED_TOKENS, QUERY_HEADS, HEAD_SIZE), jnp.float32) * col_query
    key_direction = jax.random.truncated_normal(fragments[5], -4.0, 4.0, (PACKED_TOKENS, KEY_VALUE_HEADS, HEAD_SIZE), jnp.float32) * column_key_part
    return (query_dir * row_query, key_direction * row_key_part)


def draw_query_raw(key, part):
    return raw_pair(key)[0].astype(jnp.bfloat16)


def draw_key_raw(key, part):
    return raw_pair(key)[1].astype(jnp.bfloat16)


def gain_draw(key, salt):
    folded = jax.random.fold_in(key, salt)
    return jnp.exp(jax.random.uniform(folded, (HEAD_SIZE,), jnp.float32, math.log(0.5), math.log(2.0)))


def draw_query_gain(key, part):
    return gain_draw(key, 21)


def draw_key_gain(key, part):
    return gain_draw(key, 22)


def draw_output_gradient(key, part):
    fragments = jax.random.split(jax.random.fold_in(key, 31), 1)
    position = jnp.arange(PACKED_TOKENS, dtype=jnp.float32)[:, None, None] / PACKED_TOKENS
    rising = jnp.exp(math.log(3.0) * position)
    noise = jax.random.truncated_normal(fragments[0], -4.0, 4.0, (PACKED_TOKENS, QUERY_HEADS, HEAD_SIZE), jnp.float32)
    return (noise * rising).astype(jnp.bfloat16)


def block_levels(stream_key, shape, pieces, smallest, top_value):
    loudness, own = 1.0, jax.random.fold_in(stream_key, 6)
    for dim, blocks in pieces:
        heights = jnp.exp(jax.random.uniform(jax.random.fold_in(own, dim), (blocks,), jnp.float32, smallest / len(pieces), top_value / len(pieces)))
        loudness = loudness * jnp.repeat(heights, shape[dim] // blocks).reshape([-1 if axis == dim else 1 for axis in range(len(shape))])
    return loudness


def profile(count, total, limit, lean):
    portions = [(1 << 20) // math.isqrt(standing ** lean) + 1 for standing in range(2, count + 1)]
    rest, counts = total - limit - (count - 1), [1] * (count - 1)
    while rest > 0:
        free = [i for i in range(count - 1) if counts[i] < limit]
        mass, budget = sum([portions[i] for i in free]), rest
        for i in free:
            extra = min(limit - counts[i], max(1, budget * portions[i] // mass), rest)
            counts[i] = counts[i] + extra
            rest = rest - extra
    return np.array([limit] + counts)


def uneven_parts(own_key, number_of, total, reach, slope):
    if number_of == 2:
        one = jax.random.randint(own_key, (), max(1, total - reach), min(reach, total - 1) + 1)
        return jnp.stack([one, total - one])
    lengths = jnp.asarray(profile(number_of, total, reach, slope), jnp.int32)
    couples = (number_of - 1) // 2
    giver, sink = lengths[1:1 + 2 * couples:2], lengths[2:2 + 2 * couples:2]
    room = jnp.minimum(giver - 1, reach - sink)
    passed = jax.random.randint(jax.random.fold_in(own_key, 1), (couples,), 0, 1 << 20) % (room + 1)
    lengths = lengths.at[1:1 + 2 * couples:2].set(giver - passed).at[2:2 + 2 * couples:2].set(sink + passed)
    return lengths[jax.random.permutation(jax.random.fold_in(own_key, 2), number_of)]


def gaussian(stream_key, extent, scale, most, cuts=(), held_as=jnp.bfloat16):
    level = block_levels(stream_key, extent, cuts, -0.22, 0.18) if cuts else 1.0
    values = jax.random.normal(stream_key, extent, jnp.float32) * scale * level
    return jnp.minimum(jnp.maximum(values, -most), most).astype(held_as)


def setup_inputs(seed: int = 0) -> dict:
    keys = jax.random.split(jax.random.key(seed), 8)
    query_raw = draw_query_raw(jax.random.fold_in(keys[7], 71), 0)
    key_raw = draw_key_raw(jax.random.fold_in(keys[7], 71), 0)
    value_matrix = gaussian(keys[2], (PACKED_TOKENS, KEY_VALUE_HEADS, HEAD_SIZE), 1.0, 6.0, ((0, 128), (1, 2)))
    query_gain = draw_query_gain(jax.random.fold_in(keys[7], 71), 0)
    key_gain = draw_key_gain(jax.random.fold_in(keys[7], 71), 0)
    doc_ids = jnp.searchsorted(jnp.cumsum(uneven_parts(keys[5], N_CTX // 2, PACKED_TOKENS, 2 * LOOKBACK_SPAN, 2)), jnp.arange(PACKED_TOKENS), side="right").astype(jnp.int32)
    output_gradient = draw_output_gradient(jax.random.fold_in(keys[7], 71), 0)
    return {"query_raw": query_raw, "key_raw": key_raw, "value_matrix": value_matrix, "query_gain": query_gain, "key_gain": key_gain, "doc_ids": doc_ids, "output_gradient": output_gradient}


epsilon = 1e-06
score_scale = 168.0 ** (-0.5)
masked_score = -1e+30

def normalize(raw_rows, gain_values):
    widened = raw_rows.astype(jnp.float32)
    inverse = lax.rsqrt(lax.optimization_barrier(jnp.mean(widened * widened, axis=-1, keepdims=True)) + epsilon)
    unit_rows = widened * inverse
    return ((unit_rows * gain_values).astype(jnp.bfloat16), unit_rows, inverse)

def normalize_back(normed_grad, unit_rows, inverse, gain_values):
    scaled = normed_grad * gain_values
    return inverse * (scaled - unit_rows * lax.optimization_barrier(jnp.mean(scaled * unit_rows, axis=-1, keepdims=True)))

def rounded(values_in):
    return lax.optimization_barrier(values_in.astype(jnp.bfloat16)).astype(jnp.float32)

def reference(query_raw, key_raw, value_matrix, query_gain, key_gain, doc_ids, output_gradient):
    query_group_width = QUERY_HEADS // KEY_VALUE_HEADS
    query_matrix, query_unit, query_inv = normalize(query_raw, query_gain)
    key_matrix, key_unit, key_inv = normalize(key_raw, key_gain)
    padded_keys = jnp.concatenate([jnp.zeros((LOOKBACK_SPAN, KEY_VALUE_HEADS, HEAD_SIZE), jnp.bfloat16), key_matrix], 0)
    padded_values = jnp.concatenate([jnp.zeros((LOOKBACK_SPAN, KEY_VALUE_HEADS, HEAD_SIZE), jnp.bfloat16), value_matrix], 0)
    doc_padded = jnp.concatenate([jnp.full((LOOKBACK_SPAN,), -1, jnp.int32), doc_ids])
    key_span = LOOKBACK_SPAN + TOKENS_PER_SHARD
    block_count = PACKED_TOKENS // TOKENS_PER_SHARD

    def one_block(carried, block_id):
        key_acc, value_acc = carried
        first_row_index = (block_id * TOKENS_PER_SHARD).astype(jnp.int32)
        query_slab = lax.dynamic_slice_in_dim(query_matrix, first_row_index, TOKENS_PER_SHARD, 0).astype(jnp.float32).reshape(TOKENS_PER_SHARD, KEY_VALUE_HEADS, query_group_width, HEAD_SIZE)
        gradient_slab = lax.dynamic_slice_in_dim(output_gradient, first_row_index, TOKENS_PER_SHARD, 0).astype(jnp.float32).reshape(TOKENS_PER_SHARD, KEY_VALUE_HEADS, query_group_width, HEAD_SIZE)
        key_block = lax.dynamic_slice_in_dim(padded_keys, first_row_index, key_span, 0).astype(jnp.float32)
        value_block = lax.dynamic_slice_in_dim(padded_values, first_row_index, key_span, 0).astype(jnp.float32)
        query_doc = lax.dynamic_slice_in_dim(doc_ids, first_row_index, TOKENS_PER_SHARD, 0)
        key_doc = lax.dynamic_slice_in_dim(doc_padded, first_row_index, key_span, 0)
        query_pos = first_row_index + jnp.arange(TOKENS_PER_SHARD, dtype=jnp.int32)
        key_pos = first_row_index - LOOKBACK_SPAN + jnp.arange(key_span, dtype=jnp.int32)
        before = query_pos[:, None] - key_pos[None, :]
        allowed = (before >= 0) & (before < LOOKBACK_SPAN) & (key_pos[None, :] >= 0) & (query_doc[:, None] == key_doc[None, :])
        scores = jnp.einsum('tgjd,sgd->gjts', query_slab, key_block) * score_scale
        scores = jnp.where(allowed, scores, masked_score)
        peak_score = lax.optimization_barrier(jnp.max(scores, axis=-1, keepdims=True))
        exp_total = lax.optimization_barrier(jnp.sum(jnp.exp(scores - peak_score), axis=-1, keepdims=True))
        log_total = peak_score + jnp.log(exp_total)
        attend = rounded(jnp.exp(scores - log_total))
        out_rows = rounded(jnp.einsum('gjts,sgd->gjtd', attend, value_block))
        row_dots = jnp.einsum('tgjd,gjtd->gjt', gradient_slab, out_rows)
        prob_grad = jnp.einsum('tgjd,sgd->gjts', gradient_slab, value_block)
        score_grad = rounded(attend * (prob_grad - row_dots[..., None]))
        query_term = jnp.einsum('gjts,sgd->tgjd', score_grad, key_block) * score_scale
        key_term = jnp.einsum('gjts,tgjd->sgd', score_grad, query_slab) * score_scale
        value_term = jnp.einsum('gjts,tgjd->sgd', attend, gradient_slab)
        key_old = lax.dynamic_slice_in_dim(key_acc, first_row_index, key_span, 0)
        value_old = lax.dynamic_slice_in_dim(value_acc, first_row_index, key_span, 0)
        key_acc = lax.dynamic_update_slice_in_dim(key_acc, key_old + key_term, first_row_index, 0)
        value_acc = lax.dynamic_update_slice_in_dim(value_acc, value_old + value_term, first_row_index, 0)
        return ((key_acc, value_acc), query_term.reshape(TOKENS_PER_SHARD, QUERY_HEADS, HEAD_SIZE))
    starting_value = (jnp.zeros((PACKED_TOKENS + LOOKBACK_SPAN, KEY_VALUE_HEADS, HEAD_SIZE), jnp.float32), jnp.zeros((PACKED_TOKENS + LOOKBACK_SPAN, KEY_VALUE_HEADS, HEAD_SIZE), jnp.float32))
    (key_acc, value_acc), query_terms = lax.scan(one_block, starting_value, jnp.arange(block_count, dtype=jnp.int32))
    query_normed_grad = query_terms.reshape(PACKED_TOKENS, QUERY_HEADS, HEAD_SIZE)
    key_normed_grad = key_acc[LOOKBACK_SPAN:]
    value_grad = value_acc[LOOKBACK_SPAN:].astype(jnp.bfloat16)
    query_grad = normalize_back(query_normed_grad, query_unit, query_inv, query_gain).astype(jnp.bfloat16)
    key_grad = normalize_back(key_normed_grad, key_unit, key_inv, key_gain).astype(jnp.bfloat16)
    query_gain_grad = lax.optimization_barrier(jnp.sum(query_normed_grad * query_unit, axis=(0, 1))) / PACKED_TOKENS
    key_gain_grad = lax.optimization_barrier(jnp.sum(key_normed_grad * key_unit, axis=(0, 1))) / PACKED_TOKENS
    return (query_grad, key_grad, value_grad, query_gain_grad, key_gain_grad)
```

```python
import functools
import jax
import jax.numpy as jnp
from jax import lax
from jax.experimental import pallas as pl
from jax.experimental.pallas import tpu as pltpu
from jax.sharding import Mesh, PartitionSpec as P

LOOKBACK_SPAN = 1024
epsilon = 1e-06
score_scale = 168.0 ** (-0.5)
exponent_scale = score_scale * 1.4426950408889634
masked_score = -1e30
F32 = jnp.float32
BF16 = jnp.bfloat16
VMEM = pl.BlockSpec(memory_space=pltpu.VMEM)


def call(body, out_shape, scratch, flops, moved, exps, *args):
    return pl.pallas_call(
        body,
        out_shape=out_shape,
        in_specs=[VMEM] * len(args),
        out_specs=jax.tree.map(lambda _: VMEM, out_shape),
        scratch_shapes=scratch,
        compiler_params=pltpu.CompilerParams(vmem_limit_bytes=48 << 20),
        cost_estimate=pl.CostEstimate(flops=flops, bytes_accessed=moved, transcendentals=exps),
    )(*args)


def pack_body(per_owner, *refs):
    count = len(per_owner)
    sources, out_ref, wide = refs[:count], refs[count], refs[count + 1]
    slot = 0
    for source, heads in zip(sources, per_owner):
        total = source.shape[1]
        wide[:, :total, :] = source[...].astype(F32)
        for head in range(total):
            out_ref[head // heads, slot + head % heads] = wide[:, head, :].astype(BF16)
        slot += heads


def pack(owners, *sources):
    tokens, _, width = sources[0].shape
    per_owner = [source.shape[1] // owners for source in sources]
    widest = max(source.shape[1] for source in sources)
    size = sum(source.size for source in sources)
    return call(
        functools.partial(pack_body, per_owner),
        jax.ShapeDtypeStruct((owners, sum(per_owner), tokens, width), BF16),
        [pltpu.VMEM((tokens, widest, width), F32)],
        size,
        4 * size,
        0,
        *sources,
    )


def unpack_body(per_owner, in_ref, *refs):
    outs, wide = refs[:-1], refs[-1]
    owners = in_ref.shape[0]
    slot = 0
    for out_ref, heads in zip(outs, per_owner):
        total = out_ref.shape[1]
        for head in range(total):
            wide[:, head, :] = in_ref[head // heads, slot + head % heads].astype(F32)
        out_ref[...] = wide[:, :total, :].astype(BF16)
        slot += heads


def unpack(received, per_owner):
    owners, _, tokens, width = received.shape
    return call(
        functools.partial(unpack_body, per_owner),
        [jax.ShapeDtypeStruct((tokens, owners * heads, width), BF16) for heads in per_owner],
        [pltpu.VMEM((tokens, owners * max(per_owner), width), F32)],
        received.size,
        4 * received.size,
        0,
        received,
    )


def unit_and_inverse(raw):
    widened = raw.astype(F32)
    inverse = lax.rsqrt(jnp.mean(widened * widened, axis=-1, keepdims=True) + epsilon)
    return widened * inverse, inverse


def normalize_back(normed_grad, unit_rows, inverse, gain_values):
    scaled = normed_grad * gain_values
    return inverse * (scaled - unit_rows * jnp.mean(scaled * unit_rows, axis=-1, keepdims=True))


def contract_last(left, right):
    return lax.dot_general(left, right, (((1,), (1,)), ((), ())), preferred_element_type=F32)


def matmul(left, right):
    return lax.dot_general(left, right, (((1,), (0,)), ((), ())), preferred_element_type=F32)


def fold_rows(tile, combine):
    return combine(tile.reshape(tile.shape[0] // 8, 8, tile.shape[1]), axis=0)


def attend_body(
    qd_ref, own_ref, prev_ref, doc_ref, qgain_ref, kgain_ref,
    qgrad_ref, dk_own_ref, dv_own_ref, back_ref, gain_ref,
    key_rows, key_cols, value_cols, key_docs, score_buf, attend_buf, grad_buf, dk_acc, dv_acc, gain_acc,
):
    blocks, _, rows, width = qd_ref.shape
    tiles = blocks + 1
    window = tiles * rows
    query_gain = qgain_ref[...]
    key_gain = kgain_ref[...]
    for block in range(2 * blocks):
        source = prev_ref if block < blocks else own_ref
        span = slice(block * rows, (block + 1) * rows)
        unit, _ = unit_and_inverse(source[block % blocks, 0])
        normed = (unit * key_gain).astype(BF16)
        key_rows[span, :] = normed
        key_cols[:, span] = normed.T
        value_cols[:, span] = source[block % blocks, 1].T
        key_docs[span, :] = jnp.broadcast_to(doc_ref[:, span], (rows, rows)).T
    dk_acc[...] = jnp.zeros_like(dk_acc)
    dv_acc[...] = jnp.zeros_like(dv_acc)
    gain_acc[...] = jnp.zeros_like(gain_acc)

    key_index = lax.broadcasted_iota(jnp.int32, (rows, rows), 0)
    query_index = lax.broadcasted_iota(jnp.int32, (rows, rows), 1)

    def one_block(block, _):
        start = pl.multiple_of(block * rows, rows)
        own_start = pl.multiple_of((block + blocks) * rows, rows)
        query_unit, query_inverse = unit_and_inverse(qd_ref[block, 0:2].reshape(2 * rows, width))
        query = (query_unit * query_gain).astype(BF16)
        out_grad = qd_ref[block, 2:4].reshape(2 * rows, width)
        query_docs = doc_ref[:, pl.ds(own_start, rows)]
        peak = jnp.full((8, 2 * rows), masked_score, F32)
        for tile in range(tiles):
            span = pl.ds(pl.multiple_of(start + tile * rows, rows), rows)
            allowed = key_docs[span, :] == query_docs
            if tile == 0:
                allowed = allowed & (key_index > query_index)
            if tile == tiles - 1:
                allowed = allowed & (key_index <= query_index)
            scores = contract_last(key_rows[span, :], query)
            scores = jnp.concatenate(
                [
                    jnp.where(allowed, scores[:, :rows], masked_score),
                    jnp.where(allowed, scores[:, rows:], masked_score),
                ],
                axis=1,
            )
            score_buf[tile * rows:(tile + 1) * rows, :] = scores
            peak = jnp.maximum(peak, fold_rows(scores, jnp.max))
        peak = jnp.max(peak, axis=0, keepdims=True)
        total = jnp.zeros((8, 2 * rows), F32)
        for tile in range(tiles):
            local = slice(tile * rows, (tile + 1) * rows)
            powers = jnp.exp2((score_buf[local, :] - peak) * exponent_scale)
            score_buf[local, :] = powers
            total = total + fold_rows(powers, jnp.sum)
        inverse_total = 1.0 / jnp.sum(total, axis=0, keepdims=True)
        for tile in range(tiles):
            local = slice(tile * rows, (tile + 1) * rows)
            attend_buf[local, :] = (score_buf[local, :] * inverse_total).astype(BF16)
        out_cols = matmul(value_cols[:, pl.ds(start, window)], attend_buf[...])
        out_grad_cols = jnp.concatenate(
            [out_grad[:rows].T, out_grad[rows:].T], axis=1
        ).astype(F32)
        row_dots = jnp.sum(
            out_grad_cols * out_cols.astype(BF16).astype(F32), axis=0, keepdims=True
        )
        for tile in range(tiles):
            local = slice(tile * rows, (tile + 1) * rows)
            source_block = block + tile
            value_rows = value_cols[:, pl.ds(pl.multiple_of(start + tile * rows, rows), rows)]
            prob_grad = lax.dot_general(
                value_rows, out_grad_cols.astype(BF16), (((0,), (0,)), ((), ())),
                preferred_element_type=F32,
            )
            grad_buf[local, :] = (
                attend_buf[local, :].astype(F32) * (prob_grad - row_dots)
            ).astype(BF16)
        reach = pl.ds(start, window)
        dk_acc[reach, :] += matmul(grad_buf[...], query)
        dv_acc[reach, :] += matmul(attend_buf[...], out_grad)
        query_cols = matmul(key_cols[:, reach], grad_buf[...])
        normed_grad = (
            jnp.concatenate([query_cols[:, :rows].T, query_cols[:, rows:].T], axis=0) * score_scale
        )
        gain_acc[0:8, :] += fold_rows(normed_grad * query_unit, jnp.sum)
        query_grad = normalize_back(normed_grad, query_unit, query_inverse, query_gain)
        qgrad_ref[block] = query_grad.astype(BF16).reshape(2, rows, width)
        return 0

    lax.fori_loop(0, blocks, one_block, 0)

    for block in range(2 * blocks):
        source = prev_ref if block < blocks else own_ref
        span = slice(block * rows, (block + 1) * rows)
        unit, _ = unit_and_inverse(source[block % blocks, 0])
        key_part = dk_acc[span, :] * score_scale
        gain_acc[8:16, :] += fold_rows(key_part * unit, jnp.sum)
        if block < blocks:
            back_ref[block, 0] = key_part.astype(BF16)
            back_ref[block, 1] = dv_acc[span, :].astype(BF16)
        else:
            dk_own_ref[block - blocks] = key_part
            dv_own_ref[block - blocks] = dv_acc[span, :]
    gain_ref[0:1, :] = jnp.sum(gain_acc[0:8, :], axis=0, keepdims=True)
    gain_ref[1:2, :] = jnp.sum(gain_acc[8:16, :], axis=0, keepdims=True)


def attend(queries, own, prev, docs, query_gain, key_gain):
    blocks, _, rows, width = queries.shape
    window = (blocks + 1) * rows
    tile_flops = 2 * window * 2 * rows * width
    return call(
        attend_body,
        [
            jax.ShapeDtypeStruct((blocks, 2, rows, width), BF16),
            jax.ShapeDtypeStruct((blocks, rows, width), F32),
            jax.ShapeDtypeStruct((blocks, rows, width), F32),
            jax.ShapeDtypeStruct((blocks, 2, rows, width), BF16),
            jax.ShapeDtypeStruct((2, width), F32),
        ],
        [
            pltpu.VMEM((2 * blocks * rows, width), BF16),
            pltpu.VMEM((width, 2 * blocks * rows), BF16),
            pltpu.VMEM((width, 2 * blocks * rows), BF16),
            pltpu.VMEM((2 * blocks * rows, rows), jnp.int32),
            pltpu.VMEM((window, 2 * rows), F32),
            pltpu.VMEM((window, 2 * rows), BF16),
            pltpu.VMEM((window, 2 * rows), BF16),
            pltpu.VMEM((2 * blocks * rows, width), F32),
            pltpu.VMEM((2 * blocks * rows, width), F32),
            pltpu.VMEM((16, width), F32),
        ],
        6 * blocks * tile_flops,
        8 * queries.size,
        blocks * window * 2 * rows,
        queries, own, prev, docs, query_gain, key_gain,
    )


def finish_keys_body(own_ref, dk_ref, dv_ref, back_ref, kgain_ref, out_ref):
    key_gain = kgain_ref[...]
    for block in range(own_ref.shape[0]):
        unit, inverse = unit_and_inverse(own_ref[block, 0])
        key_total = dk_ref[block] + back_ref[block, 0].astype(F32)
        value_total = dv_ref[block] + back_ref[block, 1].astype(F32)
        out_ref[block, 0] = normalize_back(key_total, unit, inverse, key_gain).astype(BF16)
        out_ref[block, 1] = value_total.astype(BF16)


def finish_keys(own, dk_own, dv_own, back, key_gain):
    return call(
        finish_keys_body,
        jax.ShapeDtypeStruct(own.shape, BF16),
        [],
        10 * own.size,
        8 * own.size,
        0,
        own, dk_own, dv_own, back, key_gain,
    )


def per_device(ring_axes, query_raw, key_raw, value_matrix, query_gain, key_gain, doc_ids, output_gradient):
    ring_size = lax.axis_size("z")
    rings = lax.axis_size(ring_axes)
    rows = query_raw.shape[0]
    width = query_raw.shape[2]
    span = ring_size * rows
    forward = [(ring, ring + 1) for ring in range(rings - 1)]
    backward = [(ring + 1, ring) for ring in range(rings - 1)]
    query_gain = query_gain.reshape(1, width)
    key_gain = key_gain.reshape(1, width)

    def exchange(value):
        return lax.all_to_all(value, "z", 0, 0, tiled=True)

    own = exchange(pack(ring_size, key_raw, value_matrix))
    prev = lax.ppermute(own, ring_axes, forward)
    queries = exchange(pack(ring_size, query_raw, output_gradient))
    doc_padded = jnp.concatenate([jnp.full((span,), -1, jnp.int32), doc_ids])
    docs = lax.dynamic_slice_in_dim(
        doc_padded, lax.axis_index(ring_axes) * span, 2 * span, 0
    ).reshape(1, 2 * span)
    query_back, dk_own, dv_own, back, gain_part = attend(
        queries, own, prev, docs, query_gain, key_gain
    )
    got_back = lax.ppermute(back, ring_axes, backward)
    (query_grad,) = unpack(exchange(query_back), [2])
    sent = finish_keys(own, dk_own, dv_own, got_back, key_gain)
    key_grad, value_grad = unpack(exchange(sent), [1, 1])
    gain_sum = gain_part
    for axis in ("kv", "z", "y", "x"):
        gain_sum = lax.psum(gain_sum, axis)
    gain_sum = gain_sum / doc_ids.shape[0]
    return query_grad, key_grad, value_grad, gain_sum[0], gain_sum[1]


def solution(mesh):
    ring_size = LOOKBACK_SPAN // 128
    grid = Mesh(mesh.devices.reshape(4, 4, ring_size, 2), ("x", "y", "z", "kv"))
    split = P(("x", "y", "z"), "kv", None)
    return jax.shard_map(
        functools.partial(per_device, ("x", "y")),
        mesh=grid,
        in_specs=(split, split, split, P(), P(), P(), split),
        out_specs=(split, split, split, P(), P()),
        check_vma=False,
    )
```

```python
import functools
import jax
import jax.numpy as jnp
from jax import lax
from jax.experimental import pallas as pl
from jax.experimental.pallas import tpu as pltpu
from jax.sharding import Mesh, PartitionSpec as P

LOOKBACK_SPAN = 1024
epsilon = 1e-06
score_scale = 168.0 ** (-0.5)
exponent_scale = score_scale * 1.4426950408889634
masked_score = -1e30
F32 = jnp.float32
BF16 = jnp.bfloat16
TAIL_ROWS = 16
VMEM_BYTES = 8 << 20
HBM = pl.BlockSpec(memory_space=pltpu.HBM)
VMEM = pl.BlockSpec(memory_space=pltpu.VMEM)


def call(body, out_shape, scratch, flops, moved, exps, *args, vmem_bytes=VMEM_BYTES):
    return pl.pallas_call(
        body,
        out_shape=out_shape,
        in_specs=[VMEM] * len(args),
        out_specs=jax.tree.map(
            lambda out: HBM if getattr(out, "memory_space", None) == pltpu.HBM else VMEM,
            out_shape,
        ),
        scratch_shapes=scratch,
        compiler_params=pltpu.CompilerParams(vmem_limit_bytes=vmem_bytes),
        cost_estimate=pl.CostEstimate(flops=flops, bytes_accessed=moved, transcendentals=exps),
    )(*args)


def pack_body(per_owner, passed, *refs):
    count = len(per_owner)
    sources, extras, refs = refs[:count], refs[count:count + passed], refs[count + passed:]
    out_ref, extra_outs = refs[0], refs[1:1 + passed]
    staged, wide, sems = refs[1 + passed:-2], refs[-2], refs[-1]
    copies = [
        pltpu.make_async_copy(source, stage, sems.at[index])
        for index, (source, stage) in enumerate(zip(sources, staged))
    ]
    for copy in copies:
        copy.start()
    for extra, extra_out in zip(extras, extra_outs):
        extra_out[...] = extra[...]
    slot = 0
    for copy, stage, heads in zip(copies, staged, per_owner):
        copy.wait()
        tokens, total, width = stage.shape
        wide[...] = stage[...].astype(F32).reshape(tokens * total, width)
        for head in range(total):
            out_ref[head // heads, slot + head % heads] = wide[
                pl.ds(head, tokens, stride=total), :
            ].astype(BF16)
        slot += heads


def pack(owners, sources, *extras):
    tokens, total, width = sources[0].shape
    per_owner = [source.shape[1] // owners for source in sources]
    size = sum(source.size for source in sources)
    return pl.pallas_call(
        functools.partial(pack_body, per_owner, len(extras)),
        out_shape=[
            jax.ShapeDtypeStruct((owners, sum(per_owner), tokens, width), BF16),
        ] + [jax.ShapeDtypeStruct(extra.shape, extra.dtype) for extra in extras],
        in_specs=[pl.BlockSpec(memory_space=pltpu.HBM)] * len(sources) + [VMEM] * len(extras),
        out_specs=[VMEM] * (1 + len(extras)),
        scratch_shapes=[pltpu.VMEM(source.shape, BF16) for source in sources] + [
            pltpu.VMEM((tokens * total, width), F32),
            pltpu.SemaphoreType.DMA((len(sources),)),
        ],
        compiler_params=pltpu.CompilerParams(vmem_limit_bytes=VMEM_BYTES),
        cost_estimate=pl.CostEstimate(flops=size, bytes_accessed=4 * size, transcendentals=0),
    )(*[pltpu.with_memory_space_constraint(source, pltpu.HBM) for source in sources], *extras)


def unpack_queries_body(in_ref, out_ref, wide):
    owners = in_ref.shape[0]
    tokens, total, width = out_ref.shape
    heads = total // owners
    for head in range(total):
        first = (head % heads) * tokens
        wide[pl.ds(head, tokens, stride=total), :] = (
            in_ref[head // heads, first:first + tokens, :].astype(F32)
        )
    out_ref[...] = wide[...].reshape(tokens, total, width).astype(BF16)


def unpack_queries(received, tokens):
    owners, rows, width = received.shape
    heads = owners * (rows // tokens)
    return call(
        unpack_queries_body,
        jax.ShapeDtypeStruct((tokens, heads, width), BF16),
        [pltpu.VMEM((tokens * heads, width), F32)],
        received.size, 4 * received.size, 0, received,
    )


def unpack_gains_body(in_ref, gain_ref):
    owners, rows, _ = in_ref.shape
    pieces = in_ref[0, rows - TAIL_ROWS:, :].astype(F32)
    for owner in range(1, owners):
        pieces = pieces + in_ref[owner, rows - TAIL_ROWS:, :].astype(F32)
    for row in range(2):
        gain_ref[row:row + 1, :] = jnp.sum(pieces[3 * row:3 * row + 3], axis=0, keepdims=True)


def unpack_gains(received):
    width = received.shape[-1]
    return call(
        unpack_gains_body,
        jax.ShapeDtypeStruct((2, width), F32),
        [], 64 * width, 64 * width, 0, received,
    )


def unpack_keys_body(in_ref, key_out, value_out, wide):
    tokens, owners, width = key_out.shape
    for slot, out_ref in enumerate((key_out, value_out)):
        for head in range(owners):
            wide[slot, pl.ds(head, tokens, stride=owners), :] = in_ref[head, slot].astype(F32)
        out_ref[...] = wide[slot].reshape(tokens, owners, width).astype(BF16)


def unpack_keys(received):
    owners, _, tokens, width = received.shape
    shape = (tokens, owners, width)
    return call(
        unpack_keys_body,
        [jax.ShapeDtypeStruct(shape, BF16)] * 2,
        [pltpu.VMEM((2, tokens * owners, width), F32)],
        received.size, 4 * received.size, 0, received,
    )


def unit_and_inverse(raw):
    widened = raw.astype(F32)
    inverse = lax.rsqrt(jnp.mean(widened * widened, axis=-1, keepdims=True) + epsilon)
    return widened * inverse, inverse


def normalize_back(normed_grad, unit_rows, inverse, gain_values):
    scaled = normed_grad * gain_values
    return inverse * (scaled - unit_rows * jnp.mean(scaled * unit_rows, axis=-1, keepdims=True))


def contract_last(left, right):
    return lax.dot_general(left, right, (((1,), (1,)), ((), ())), preferred_element_type=F32)


def matmul(left, right):
    return lax.dot_general(left, right, (((1,), (0,)), ((), ())), preferred_element_type=F32)


def fold_rows(tile, combine):
    return combine(tile.reshape(tile.shape[0] // 8, 8, tile.shape[1]), axis=0)


def three_pieces(value):
    high = value.astype(BF16)
    rest = value - high.astype(F32)
    middle = rest.astype(BF16)
    return [high, middle, (rest - middle.astype(F32)).astype(BF16)]


def attend_body(
    qd_ref, own_ref, prev_ref, doc_ref, both_gains_ref,
    qgrad_ref, dk_own_ref, dv_own_ref, back_ref,
    key_rows, value_rows, key_cols, value_cols, key_docs,
    score_buf, power_buf, grad_buf, dk_acc, dv_acc, gain_acc, back_buf, back_sem,
):
    blocks, _, rows, width = qd_ref.shape
    tiles = blocks + 1
    window = tiles * rows
    query_gain = both_gains_ref[0:1, :]
    key_gain = both_gains_ref[1:2, :]
    for block in range(2 * blocks):
        source = prev_ref if block < blocks else own_ref
        span = slice(block * rows, (block + 1) * rows)
        unit, _ = unit_and_inverse(source[block % blocks, 0])
        normed = (unit * key_gain).astype(BF16)
        values = source[block % blocks, 1]
        key_rows[span, :] = normed
        value_rows[span, :] = values
        key_cols[:, span] = normed.T
        value_cols[:, span] = values.T
        key_docs[span, :] = jnp.broadcast_to(doc_ref[:, span], (rows, rows)).T
    dk_acc[...] = jnp.zeros_like(dk_acc)
    dv_acc[...] = jnp.zeros_like(dv_acc)
    gain_acc[...] = jnp.zeros_like(gain_acc)

    back_copy = pltpu.make_async_copy(back_buf, back_ref, back_sem)
    key_index = lax.broadcasted_iota(jnp.int32, (rows, rows), 0)
    query_index = lax.broadcasted_iota(jnp.int32, (rows, rows), 1)
    CHUNK = 1

    def powers_of(block):
        slot = block % 2
        query_unit, query_inverse = unit_and_inverse(qd_ref[block, 0:2].reshape(2 * rows, width))
        query = (query_unit * query_gain).astype(BF16)
        query_docs = doc_ref[:, (block + blocks) * rows:(block + blocks + 1) * rows]
        peak = jnp.full((8, 2 * rows), masked_score, F32)
        for first in range(0, tiles, CHUNK):
            lead = (block + first) * rows
            raw = contract_last(key_rows[lead:lead + CHUNK * rows, :], query)
            for tile in range(first, first + CHUNK):
                span = slice((block + tile) * rows, (block + tile + 1) * rows)
                allowed = key_docs[span, :] == query_docs
                if tile == 0:
                    allowed = allowed & (key_index > query_index)
                if tile == tiles - 1:
                    allowed = allowed & (key_index <= query_index)
                scores = raw[(tile - first) * rows:(tile - first + 1) * rows]
                scores = jnp.concatenate(
                    [
                        jnp.where(allowed, scores[:, :rows], masked_score),
                        jnp.where(allowed, scores[:, rows:], masked_score),
                    ],
                    axis=1,
                )
                score_buf[slot, tile * rows:(tile + 1) * rows, :] = scores
                peak = jnp.maximum(peak, fold_rows(scores, jnp.max))
        peak = jnp.max(peak, axis=0, keepdims=True) * exponent_scale
        total = jnp.zeros((8, 2 * rows), F32)
        for tile in range(tiles):
            local = slice(tile * rows, (tile + 1) * rows)
            powers = jnp.exp2(score_buf[slot, local, :] * exponent_scale - peak)
            power_buf[slot, local, :] = powers.astype(BF16)
            total = total + fold_rows(powers, jnp.sum)
        return query_unit, query_inverse, query, 1.0 / jnp.sum(total, axis=0, keepdims=True)

    def gradients_of(block, query_unit, query_inverse, query, inverse_total):
        slot = block % 2
        reach = slice(block * rows, block * rows + window)
        out_grad = qd_ref[block, 2:4].reshape(2 * rows, width)
        out_cols = matmul(value_cols[:, reach], power_buf[slot]) * inverse_total
        out_grad_cols = jnp.concatenate(
            [out_grad[:rows].T, out_grad[rows:].T], axis=1
        ).astype(F32) * inverse_total
        row_dots = jnp.sum(
            out_grad_cols * out_cols.astype(BF16).astype(F32), axis=0, keepdims=True
        )
        scaled_cols = out_grad_cols.astype(BF16)
        scaled_rows = jnp.concatenate([scaled_cols[:, :rows].T, scaled_cols[:, rows:].T], axis=0)
        for first in range(0, tiles, CHUNK):
            local = slice(first * rows, (first + CHUNK) * rows)
            span = slice((block + first) * rows, (block + first + CHUNK) * rows)
            prob_grad = matmul(value_rows[span, :], scaled_cols)
            grad_buf[slot, local, :] = (
                power_buf[slot, local, :].astype(F32) * (prob_grad - row_dots)
            ).astype(BF16)
        dv_acc[reach, :] += matmul(power_buf[slot], scaled_rows)
        dk_acc[reach, :] += matmul(grad_buf[slot], query)
        query_cols = matmul(key_cols[:, reach], grad_buf[slot])
        normed_grad = (
            jnp.concatenate([query_cols[:, :rows].T, query_cols[:, rows:].T], axis=0) * score_scale
        )
        gain_acc[0:8, :] += fold_rows(normed_grad * query_unit, jnp.sum)
        query_grad = normalize_back(normed_grad, query_unit, query_inverse, query_gain)
        qgrad_ref[block, 0:2 * rows, :] = query_grad.astype(BF16)

    ready = powers_of(0)
    for block in range(blocks):
        upcoming = powers_of(block + 1) if block + 1 < blocks else None
        gradients_of(block, *ready)
        ready = upcoming

    for block in range(2 * blocks):
        source = prev_ref if block < blocks else own_ref
        span = slice(block * rows, (block + 1) * rows)
        unit, _ = unit_and_inverse(source[block % blocks, 0])
        key_part = dk_acc[span, :] * score_scale
        gain_acc[8:16, :] += fold_rows(key_part * unit, jnp.sum)
        if block < blocks:
            back_buf[block, 0] = key_part.astype(BF16)
            back_buf[block, 1] = dv_acc[span, :].astype(BF16)
            if block == blocks - 1:
                back_copy.start()
        else:
            dk_own_ref[block - blocks] = key_part
            dv_own_ref[block - blocks] = dv_acc[span, :]
    back_copy.wait()
    tail = []
    for first in (0, 8):
        tail += three_pieces(jnp.sum(gain_acc[first:first + 8, :], axis=0, keepdims=True))
    tail = jnp.concatenate(
        [piece.astype(F32) for piece in tail] + [jnp.zeros((10, width), F32)], axis=0
    ).astype(BF16)
    for block in range(blocks):
        qgrad_ref[block, 2 * rows:, :] = tail


def attend(queries, own, prev, docs, gains):
    blocks, _, rows, width = own.shape
    window = (blocks + 1) * rows
    tile_flops = 2 * window * 2 * rows * width
    return call(
        attend_body,
        [
            jax.ShapeDtypeStruct((blocks, 2 * rows + TAIL_ROWS, width), BF16),
            jax.ShapeDtypeStruct((blocks, rows, width), F32),
            jax.ShapeDtypeStruct((blocks, rows, width), F32),
            pltpu.HBM((blocks, 2, rows, width), BF16),
        ],
        [
            pltpu.VMEM((2 * blocks * rows, width), BF16),
            pltpu.VMEM((2 * blocks * rows, width), BF16),
            pltpu.VMEM((width, 2 * blocks * rows), BF16),
            pltpu.VMEM((width, 2 * blocks * rows), BF16),
            pltpu.VMEM((2 * blocks * rows, rows), jnp.int32),
            pltpu.VMEM((2, window, 2 * rows), F32),
            pltpu.VMEM((2, window, 2 * rows), BF16),
            pltpu.VMEM((2, window, 2 * rows), BF16),
            pltpu.VMEM((2 * blocks * rows, width), F32),
            pltpu.VMEM((2 * blocks * rows, width), F32),
            pltpu.VMEM((16, width), F32),
            pltpu.VMEM((blocks, 2, rows, width), BF16),
            pltpu.SemaphoreType.DMA,
        ],
        6 * blocks * tile_flops,
        32 * own.size,
        blocks * window * 2 * rows,
        queries, own, prev, docs, gains,
        vmem_bytes=20 << 20,
    )


def finish_keys_body(own_ref, dk_ref, dv_ref, back_ref, gains_ref, out_ref):
    key_gain = gains_ref[1:2, :]
    for block in range(own_ref.shape[0]):
        unit, inverse = unit_and_inverse(own_ref[block, 0])
        key_total = dk_ref[block] + back_ref[block, 0].astype(F32)
        value_total = dv_ref[block] + back_ref[block, 1].astype(F32)
        out_ref[block, 0] = normalize_back(key_total, unit, inverse, key_gain).astype(BF16)
        out_ref[block, 1] = value_total.astype(BF16)


def finish_keys(own, dk_own, dv_own, back, gains):
    return call(
        finish_keys_body,
        jax.ShapeDtypeStruct(own.shape, BF16),
        [], 10 * own.size, 8 * own.size, 0,
        own, dk_own, dv_own, back, gains,
    )


def shifted_terms(value, axis):
    count = lax.axis_size(axis)
    return [
        lax.ppermute(value, axis, [(i, (i + step) % count) for i in range(count)])
        for step in range(1, count)
    ]


def add_terms(value, terms):
    for term in terms:
        value = value + term
    return value


def shifted_sum(value, axis):
    return add_terms(value, shifted_terms(value, axis))


def per_device(ring_axes, query_raw, key_raw, value_matrix, query_gain, key_gain, doc_ids, output_gradient):
    ring_size = lax.axis_size("z")
    rings = lax.axis_size(ring_axes)
    rows = query_raw.shape[0]
    span = ring_size * rows
    forward = [(ring, ring + 1) for ring in range(rings - 1)]
    backward = [(ring + 1, ring) for ring in range(rings - 1)]

    def exchange(value):
        return lax.all_to_all(value, "z", 0, 0, tiled=True)

    doc_padded = jnp.concatenate([jnp.full((span,), -1, jnp.int32), doc_ids])
    docs = lax.dynamic_slice_in_dim(
        doc_padded, lax.axis_index(ring_axes) * span, 2 * span, 0
    ).reshape(1, 2 * span)
    (sent_keys,) = pack(ring_size, (key_raw, value_matrix))
    own = exchange(sent_keys)
    prev = lax.ppermute(own, ring_axes, forward)
    sent_queries, gains = pack(
        ring_size, (query_raw, output_gradient), jnp.stack([query_gain, key_gain])
    )
    queries = exchange(sent_queries)
    query_back, dk_own, dv_own, back = attend(queries, own, prev, docs, gains)
    got_back = lax.ppermute(back, ring_axes, backward)
    got_queries = exchange(query_back)
    query_grad = unpack_queries(got_queries, rows)
    gain_sum = shifted_sum(unpack_gains(got_queries), "kv")
    got_back, gain_sum = lax.optimization_barrier((got_back, gain_sum))
    got_keys = exchange(finish_keys(own, dk_own, dv_own, got_back, gains))
    gain_sum = shifted_sum(gain_sum, "y")
    key_grad, value_grad = unpack_keys(got_keys)
    terms = shifted_terms(gain_sum, "x")
    key_grad, terms = lax.optimization_barrier((key_grad, terms))
    gain_sum = add_terms(gain_sum, terms) / doc_ids.shape[0]
    return query_grad, key_grad, value_grad, gain_sum[0], gain_sum[1]


def solution(mesh):
    ring_size = LOOKBACK_SPAN // 128
    grid = Mesh(mesh.devices.reshape(4, 4, ring_size, 2), ("x", "y", "z", "kv"))
    split = P(("x", "y", "z"), "kv", None)
    return jax.shard_map(
        functools.partial(per_device, ("x", "y")),
        mesh=grid,
        in_specs=(split, split, split, P(), P(), P(), split),
        out_specs=(split, split, split, P(), P()),
        check_vma=False,
    )
```

```python
import functools
import jax
import jax.numpy as jnp
from jax import lax
from jax.experimental import pallas as pl
from jax.experimental.pallas import tpu as pltpu
from jax.sharding import Mesh, PartitionSpec as P

LOOKBACK_SPAN = 1024
epsilon = 1e-06
score_scale = 168.0 ** (-0.5)
exponent_scale = score_scale * 1.4426950408889634
masked_score = -1e30
F32 = jnp.float32
BF16 = jnp.bfloat16
TAIL_ROWS = 16
VMEM_BYTES = 8 << 20
SMEM = pl.BlockSpec(memory_space=pltpu.SMEM)
HBM = pl.BlockSpec(memory_space=pltpu.HBM)
VMEM = pl.BlockSpec(memory_space=pltpu.VMEM)


def call(body, out_shape, scratch, flops, moved, exps, *args, vmem_bytes=VMEM_BYTES):
    return pl.pallas_call(
        body,
        out_shape=out_shape,
        in_specs=[VMEM] * len(args),
        out_specs=jax.tree.map(
            lambda out: HBM if getattr(out, "memory_space", None) == pltpu.HBM else VMEM,
            out_shape,
        ),
        scratch_shapes=scratch,
        compiler_params=pltpu.CompilerParams(vmem_limit_bytes=vmem_bytes),
        cost_estimate=pl.CostEstimate(flops=flops, bytes_accessed=moved, transcendentals=exps),
    )(*args)


def pack_body(per_owner, passed, *refs):
    count = len(per_owner)
    sources, extras, refs = refs[:count], refs[count:count + passed], refs[count + passed:]
    out_ref, extra_outs = refs[0], refs[1:1 + passed]
    staged, wide, sems = refs[1 + passed:-2], refs[-2], refs[-1]
    copies = [
        pltpu.make_async_copy(source, stage, sems.at[index])
        for index, (source, stage) in enumerate(zip(sources, staged))
    ]
    for copy in copies:
        copy.start()
    for extra, extra_out in zip(extras, extra_outs):
        extra_out[...] = extra[...]
    slot = 0
    for copy, stage, heads in zip(copies, staged, per_owner):
        copy.wait()
        tokens, total, width = stage.shape
        wide[...] = stage[...].astype(F32).reshape(tokens * total, width)
        for head in range(total):
            out_ref[head // heads, slot + head % heads] = wide[
                pl.ds(head, tokens, stride=total), :
            ].astype(BF16)
        slot += heads


def pack(owners, sources, *extras):
    tokens, total, width = sources[0].shape
    per_owner = [source.shape[1] // owners for source in sources]
    size = sum(source.size for source in sources)
    return pl.pallas_call(
        functools.partial(pack_body, per_owner, len(extras)),
        out_shape=[
            jax.ShapeDtypeStruct((owners, sum(per_owner), tokens, width), BF16),
        ] + [jax.ShapeDtypeStruct(extra.shape, extra.dtype) for extra in extras],
        in_specs=[pl.BlockSpec(memory_space=pltpu.HBM)] * len(sources) + [VMEM] * len(extras),
        out_specs=[VMEM] * (1 + len(extras)),
        scratch_shapes=[pltpu.VMEM(source.shape, BF16) for source in sources] + [
            pltpu.VMEM((tokens * total, width), F32),
            pltpu.SemaphoreType.DMA((len(sources),)),
        ],
        compiler_params=pltpu.CompilerParams(vmem_limit_bytes=VMEM_BYTES),
        cost_estimate=pl.CostEstimate(flops=size, bytes_accessed=4 * size, transcendentals=0),
    )(*[pltpu.with_memory_space_constraint(source, pltpu.HBM) for source in sources], *extras)


def pack_apart_body(place_ref, key_ref, value_ref, *refs):
    outs, staged, wide, sems = refs[:-4], refs[-4:-2], refs[-2], refs[-1]
    copies = [
        pltpu.make_async_copy(source, stage, sems.at[index])
        for index, (source, stage) in enumerate(zip((key_ref, value_ref), staged))
    ]
    for copy in copies:
        copy.start()
    owners = len(outs)
    for slot, (copy, stage) in enumerate(zip(copies, staged)):
        copy.wait()
        tokens, total, width = stage.shape
        wide[...] = stage[...].astype(F32).reshape(tokens * total, width)
        for step, out_ref in enumerate(outs):
            head = (place_ref[0] + step) % owners
            out_ref[slot] = wide[pl.ds(head, tokens, stride=total), :].astype(BF16)


def pack_apart(place, keys, values):
    tokens, heads, width = keys.shape
    return pl.pallas_call(
        pack_apart_body,
        out_shape=[jax.ShapeDtypeStruct((2, tokens, width), BF16)] * heads,
        in_specs=[SMEM, HBM, HBM],
        out_specs=[VMEM] * heads,
        scratch_shapes=[pltpu.VMEM(keys.shape, BF16)] * 2 + [
            pltpu.VMEM((tokens * heads, width), F32),
            pltpu.SemaphoreType.DMA((2,)),
        ],
        compiler_params=pltpu.CompilerParams(vmem_limit_bytes=VMEM_BYTES),
        cost_estimate=pl.CostEstimate(
            flops=2 * keys.size, bytes_accessed=8 * keys.size, transcendentals=0
        ),
    )(
        place,
        pltpu.with_memory_space_constraint(keys, pltpu.HBM),
        pltpu.with_memory_space_constraint(values, pltpu.HBM),
    )


def gather_pieces_body(place_ref, *refs):
    pieces, out_ref = refs[:-1], refs[-1]
    owners = len(pieces)
    for step, piece in enumerate(pieces):
        out_ref[(place_ref[0] + owners - step) % owners] = piece[...]


def gather_pieces(place, pieces):
    shape = (len(pieces),) + pieces[0].shape
    size = len(pieces) * pieces[0].size
    return pl.pallas_call(
        gather_pieces_body,
        out_shape=jax.ShapeDtypeStruct(shape, BF16),
        in_specs=[SMEM] + [VMEM] * len(pieces),
        out_specs=VMEM,
        compiler_params=pltpu.CompilerParams(vmem_limit_bytes=VMEM_BYTES),
        cost_estimate=pl.CostEstimate(flops=size, bytes_accessed=4 * size, transcendentals=0),
    )(place, *pieces)


def unpack_queries_body(in_ref, out_ref, wide):
    owners = in_ref.shape[0]
    tokens, total, width = out_ref.shape
    heads = total // owners
    for head in range(total):
        first = (head % heads) * tokens
        wide[pl.ds(head, tokens, stride=total), :] = (
            in_ref[head // heads, first:first + tokens, :].astype(F32)
        )
    out_ref[...] = wide[...].reshape(tokens, total, width).astype(BF16)


def unpack_queries(received, tokens):
    owners, rows, width = received.shape
    heads = owners * (rows // tokens)
    return call(
        unpack_queries_body,
        jax.ShapeDtypeStruct((tokens, heads, width), BF16),
        [pltpu.VMEM((tokens * heads, width), F32)],
        received.size, 4 * received.size, 0, received,
    )


def unpack_gains_body(in_ref, gain_ref):
    owners, rows, _ = in_ref.shape
    pieces = in_ref[0, rows - TAIL_ROWS:, :].astype(F32)
    for owner in range(1, owners):
        pieces = pieces + in_ref[owner, rows - TAIL_ROWS:, :].astype(F32)
    for row in range(2):
        gain_ref[row:row + 1, :] = jnp.sum(pieces[3 * row:3 * row + 3], axis=0, keepdims=True)


def unpack_gains(received):
    width = received.shape[-1]
    return call(
        unpack_gains_body,
        jax.ShapeDtypeStruct((2, width), F32),
        [], 64 * width, 64 * width, 0, received,
    )


def unpack_keys_body(in_ref, key_out, value_out, wide):
    tokens, owners, width = key_out.shape
    for slot, out_ref in enumerate((key_out, value_out)):
        for head in range(owners):
            wide[slot, pl.ds(head, tokens, stride=owners), :] = in_ref[head, slot].astype(F32)
        out_ref[...] = wide[slot].reshape(tokens, owners, width).astype(BF16)


def unpack_keys(received):
    owners, _, tokens, width = received.shape
    shape = (tokens, owners, width)
    return call(
        unpack_keys_body,
        [jax.ShapeDtypeStruct(shape, BF16)] * 2,
        [pltpu.VMEM((2, tokens * owners, width), F32)],
        received.size, 4 * received.size, 0, received,
    )


def unit_and_inverse(raw):
    widened = raw.astype(F32)
    inverse = lax.rsqrt(jnp.mean(widened * widened, axis=-1, keepdims=True) + epsilon)
    return widened * inverse, inverse


def normalize_back(normed_grad, unit_rows, inverse, gain_values):
    scaled = normed_grad * gain_values
    return inverse * (scaled - unit_rows * jnp.mean(scaled * unit_rows, axis=-1, keepdims=True))


def contract_last(left, right):
    return lax.dot_general(left, right, (((1,), (1,)), ((), ())), preferred_element_type=F32)


def matmul(left, right):
    return lax.dot_general(left, right, (((1,), (0,)), ((), ())), preferred_element_type=F32)


def fold_rows(tile, combine):
    return combine(tile.reshape(tile.shape[0] // 8, 8, tile.shape[1]), axis=0)


def three_pieces(value):
    high = value.astype(BF16)
    rest = value - high.astype(F32)
    middle = rest.astype(BF16)
    return [high, middle, (rest - middle.astype(F32)).astype(BF16)]


def attend_body(
    qd_ref, own_ref, prev_ref, doc_ref, both_gains_ref,
    qgrad_ref, dk_own_ref, dv_own_ref, back_ref,
    key_rows, value_rows, key_cols, value_cols, key_docs,
    score_buf, power_buf, grad_buf, dk_acc, dv_acc, gain_acc, back_buf, back_sem,
):
    blocks, _, rows, width = qd_ref.shape
    tiles = blocks + 1
    window = tiles * rows
    query_gain = both_gains_ref[0:1, :]
    key_gain = both_gains_ref[1:2, :]
    for block in range(2 * blocks):
        source = prev_ref if block < blocks else own_ref
        span = slice(block * rows, (block + 1) * rows)
        unit, _ = unit_and_inverse(source[block % blocks, 0])
        normed = (unit * key_gain).astype(BF16)
        values = source[block % blocks, 1]
        key_rows[span, :] = normed
        value_rows[span, :] = values
        key_cols[:, span] = normed.T
        value_cols[:, span] = values.T
        key_docs[span, :] = jnp.broadcast_to(doc_ref[:, span], (rows, rows)).T
    dk_acc[...] = jnp.zeros_like(dk_acc)
    dv_acc[...] = jnp.zeros_like(dv_acc)
    gain_acc[...] = jnp.zeros_like(gain_acc)

    back_copy = pltpu.make_async_copy(back_buf, back_ref, back_sem)
    key_index = lax.broadcasted_iota(jnp.int32, (rows, rows), 0)
    query_index = lax.broadcasted_iota(jnp.int32, (rows, rows), 1)
    CHUNK = 1

    def powers_of(block):
        slot = block % 2
        query_unit, query_inverse = unit_and_inverse(qd_ref[block, 0:2].reshape(2 * rows, width))
        query = (query_unit * query_gain).astype(BF16)
        query_docs = doc_ref[:, (block + blocks) * rows:(block + blocks + 1) * rows]
        peak = jnp.full((8, 2 * rows), masked_score, F32)
        for first in range(0, tiles, CHUNK):
            lead = (block + first) * rows
            raw = contract_last(key_rows[lead:lead + CHUNK * rows, :], query)
            for tile in range(first, first + CHUNK):
                span = slice((block + tile) * rows, (block + tile + 1) * rows)
                allowed = key_docs[span, :] == query_docs
                if tile == 0:
                    allowed = allowed & (key_index > query_index)
                if tile == tiles - 1:
                    allowed = allowed & (key_index <= query_index)
                scores = raw[(tile - first) * rows:(tile - first + 1) * rows]
                scores = jnp.concatenate(
                    [
                        jnp.where(allowed, scores[:, :rows], masked_score),
                        jnp.where(allowed, scores[:, rows:], masked_score),
                    ],
                    axis=1,
                )
                score_buf[slot, tile * rows:(tile + 1) * rows, :] = scores
                peak = jnp.maximum(peak, fold_rows(scores, jnp.max))
        peak = jnp.max(peak, axis=0, keepdims=True) * exponent_scale
        total = jnp.zeros((8, 2 * rows), F32)
        for tile in range(tiles):
            local = slice(tile * rows, (tile + 1) * rows)
            powers = jnp.exp2(score_buf[slot, local, :] * exponent_scale - peak)
            power_buf[slot, local, :] = powers.astype(BF16)
            total = total + fold_rows(powers, jnp.sum)
        return query_unit, query_inverse, query, 1.0 / jnp.sum(total, axis=0, keepdims=True)

    def gradients_of(block, query_unit, query_inverse, query, inverse_total):
        slot = block % 2
        reach = slice(block * rows, block * rows + window)
        out_grad = qd_ref[block, 2:4].reshape(2 * rows, width)
        out_cols = matmul(value_cols[:, reach], power_buf[slot]) * inverse_total
        out_grad_cols = jnp.concatenate(
            [out_grad[:rows].T, out_grad[rows:].T], axis=1
        ).astype(F32) * inverse_total
        scaled_cols = out_grad_cols.astype(BF16)
        row_dots = jnp.sum(
            scaled_cols.astype(F32) * out_cols.astype(BF16).astype(F32), axis=0, keepdims=True
        )
        scaled_rows = jnp.concatenate([scaled_cols[:, :rows].T, scaled_cols[:, rows:].T], axis=0)
        for first in range(0, tiles, CHUNK):
            local = slice(first * rows, (first + CHUNK) * rows)
            span = slice((block + first) * rows, (block + first + CHUNK) * rows)
            prob_grad = matmul(value_rows[span, :], scaled_cols)
            grad_buf[slot, local, :] = (
                power_buf[slot, local, :].astype(F32) * (prob_grad - row_dots)
            ).astype(BF16)
        dv_acc[reach, :] += matmul(power_buf[slot], scaled_rows)
        dk_acc[reach, :] += matmul(grad_buf[slot], query)
        query_cols = matmul(key_cols[:, reach], grad_buf[slot])
        normed_grad = (
            jnp.concatenate([query_cols[:, :rows].T, query_cols[:, rows:].T], axis=0) * score_scale
        )
        gain_acc[0:8, :] += fold_rows(normed_grad * query_unit, jnp.sum)
        query_grad = normalize_back(normed_grad, query_unit, query_inverse, query_gain)
        qgrad_ref[block, 0:2 * rows, :] = query_grad.astype(BF16)

    ready = powers_of(0)
    for block in range(blocks):
        upcoming = powers_of(block + 1) if block + 1 < blocks else None
        gradients_of(block, *ready)
        ready = upcoming

    for block in range(2 * blocks):
        source = prev_ref if block < blocks else own_ref
        span = slice(block * rows, (block + 1) * rows)
        unit, _ = unit_and_inverse(source[block % blocks, 0])
        key_part = dk_acc[span, :] * score_scale
        gain_acc[8:16, :] += fold_rows(key_part * unit, jnp.sum)
        if block < blocks:
            back_buf[block, 0] = key_part.astype(BF16)
            back_buf[block, 1] = dv_acc[span, :].astype(BF16)
            if block == blocks - 1:
                back_copy.start()
        else:
            dk_own_ref[block - blocks] = key_part
            dv_own_ref[block - blocks] = dv_acc[span, :]
    back_copy.wait()
    tail = []
    for first in (0, 8):
        tail += three_pieces(jnp.sum(gain_acc[first:first + 8, :], axis=0, keepdims=True))
    tail = jnp.concatenate(
        [piece.astype(F32) for piece in tail] + [jnp.zeros((10, width), F32)], axis=0
    ).astype(BF16)
    for block in range(blocks):
        qgrad_ref[block, 2 * rows:, :] = tail


def attend(queries, own, prev, docs, gains):
    blocks, _, rows, width = own.shape
    window = (blocks + 1) * rows
    tile_flops = 2 * window * 2 * rows * width
    return call(
        attend_body,
        [
            jax.ShapeDtypeStruct((blocks, 2 * rows + TAIL_ROWS, width), BF16),
            jax.ShapeDtypeStruct((blocks, rows, width), F32),
            jax.ShapeDtypeStruct((blocks, rows, width), F32),
            pltpu.HBM((blocks, 2, rows, width), BF16),
        ],
        [
            pltpu.VMEM((2 * blocks * rows, width), BF16),
            pltpu.VMEM((2 * blocks * rows, width), BF16),
            pltpu.VMEM((width, 2 * blocks * rows), BF16),
            pltpu.VMEM((width, 2 * blocks * rows), BF16),
            pltpu.VMEM((2 * blocks * rows, rows), jnp.int32),
            pltpu.VMEM((2, window, 2 * rows), F32),
            pltpu.VMEM((2, window, 2 * rows), BF16),
            pltpu.VMEM((2, window, 2 * rows), BF16),
            pltpu.VMEM((2 * blocks * rows, width), F32),
            pltpu.VMEM((2 * blocks * rows, width), F32),
            pltpu.VMEM((16, width), F32),
            pltpu.VMEM((blocks, 2, rows, width), BF16),
            pltpu.SemaphoreType.DMA,
        ],
        6 * blocks * tile_flops,
        32 * own.size,
        blocks * window * 2 * rows,
        queries, own, prev, docs, gains,
        vmem_bytes=20 << 20,
    )


def finish_keys_body(own_ref, dk_ref, dv_ref, back_ref, gains_ref, out_ref):
    key_gain = gains_ref[1:2, :]
    for block in range(own_ref.shape[0]):
        unit, inverse = unit_and_inverse(own_ref[block, 0])
        key_total = dk_ref[block] + back_ref[block, 0].astype(F32)
        value_total = dv_ref[block] + back_ref[block, 1].astype(F32)
        out_ref[block, 0] = normalize_back(key_total, unit, inverse, key_gain).astype(BF16)
        out_ref[block, 1] = value_total.astype(BF16)


def finish_keys(own, dk_own, dv_own, back, gains):
    return call(
        finish_keys_body,
        jax.ShapeDtypeStruct(own.shape, BF16),
        [], 10 * own.size, 8 * own.size, 0,
        own, dk_own, dv_own, back, gains,
    )


def shifted_terms(value, axis):
    count = lax.axis_size(axis)
    return [
        lax.ppermute(value, axis, [(i, (i + step) % count) for i in range(count)])
        for step in range(1, count)
    ]


def add_terms(value, terms):
    for term in terms:
        value = value + term
    return value


def shifted_sum(value, axis):
    return add_terms(value, shifted_terms(value, axis))


def per_device(ring_axes, query_raw, key_raw, value_matrix, query_gain, key_gain, doc_ids, output_gradient):
    ring_size = lax.axis_size("z")
    rings = lax.axis_size(ring_axes)
    rows = query_raw.shape[0]
    span = ring_size * rows
    forward = [(ring, ring + 1) for ring in range(rings - 1)]
    backward = [(ring + 1, ring) for ring in range(rings - 1)]

    def exchange(value):
        return lax.all_to_all(value, "z", 0, 0, tiled=True)

    def exchange_apart(pieces):
        return [
            lax.ppermute(piece, "z", [(i, (i + step) % ring_size) for i in range(ring_size)])
            if step else piece
            for step, piece in enumerate(pieces)
        ]

    doc_padded = jnp.concatenate([jnp.full((span,), -1, jnp.int32), doc_ids])
    docs = lax.dynamic_slice_in_dim(
        doc_padded, lax.axis_index(ring_axes) * span, 2 * span, 0
    ).reshape(1, 2 * span)
    place = lax.axis_index("z").astype(jnp.int32).reshape(1)
    pieces = pack_apart(place, key_raw, value_matrix)
    pieces = exchange_apart(pieces)
    sent_queries, gains = pack(
        ring_size, (query_raw, output_gradient), jnp.stack([query_gain, key_gain])
    )
    pieces, sent_queries = lax.optimization_barrier((pieces, sent_queries))
    own = gather_pieces(place, pieces)
    prev = lax.ppermute(own, ring_axes, forward)
    queries = exchange(sent_queries)
    query_back, dk_own, dv_own, back = attend(queries, own, prev, docs, gains)
    got_back = lax.ppermute(back, ring_axes, backward)
    got_queries = exchange(query_back)
    query_grad = unpack_queries(got_queries, rows)
    gain_sum = shifted_sum(unpack_gains(got_queries), "kv")
    got_back, gain_sum = lax.optimization_barrier((got_back, gain_sum))
    got_keys = exchange(finish_keys(own, dk_own, dv_own, got_back, gains))
    gain_sum = shifted_sum(gain_sum, "y")
    key_grad, value_grad = unpack_keys(got_keys)
    terms = shifted_terms(gain_sum, "x")
    key_grad, terms = lax.optimization_barrier((key_grad, terms))
    gain_sum = add_terms(gain_sum, terms) / doc_ids.shape[0]
    return query_grad, key_grad, value_grad, gain_sum[0], gain_sum[1]


def solution(mesh):
    ring_size = LOOKBACK_SPAN // 128
    grid = Mesh(mesh.devices.reshape(4, 4, ring_size, 2), ("x", "y", "z", "kv"))
    split = P(("x", "y", "z"), "kv", None)
    return jax.shard_map(
        functools.partial(per_device, ("x", "y")),
        mesh=grid,
        in_specs=(split, split, split, P(), P(), P(), split),
        out_specs=(split, split, split, P(), P()),
        check_vma=False,
    )
```

```python
import functools
import jax
import jax.numpy as jnp
from jax import lax
from jax.experimental import pallas as pl
from jax.experimental.pallas import tpu as pltpu
from jax.sharding import Mesh, PartitionSpec as P

LOOKBACK_SPAN = 1024
epsilon = 1e-06
score_scale = 168.0 ** (-0.5)
exponent_scale = score_scale * 1.4426950408889634
masked_score = -1e30
F32 = jnp.float32
BF16 = jnp.bfloat16
TAIL_ROWS = 16
STEP_ORDER = (1, 7, 2, 6, 3, 5, 4)
VMEM_BYTES = 8 << 20
SMEM = pl.BlockSpec(memory_space=pltpu.SMEM)
HBM = pl.BlockSpec(memory_space=pltpu.HBM)
VMEM = pl.BlockSpec(memory_space=pltpu.VMEM)


def call(body, out_shape, scratch, flops, moved, exps, *args, vmem_bytes=VMEM_BYTES):
    return pl.pallas_call(
        body,
        out_shape=out_shape,
        in_specs=[VMEM] * len(args),
        out_specs=jax.tree.map(
            lambda out: HBM if getattr(out, "memory_space", None) == pltpu.HBM else VMEM,
            out_shape,
        ),
        scratch_shapes=scratch,
        compiler_params=pltpu.CompilerParams(vmem_limit_bytes=vmem_bytes),
        cost_estimate=pl.CostEstimate(flops=flops, bytes_accessed=moved, transcendentals=exps),
    )(*args)


def pack_body(per_owner, passed, *refs):
    count = len(per_owner)
    sources, extras, refs = refs[:count], refs[count:count + passed], refs[count + passed:]
    out_ref, extra_outs = refs[0], refs[1:1 + passed]
    staged, wide, sems = refs[1 + passed:-2], refs[-2], refs[-1]
    copies = [
        pltpu.make_async_copy(source, stage, sems.at[index])
        for index, (source, stage) in enumerate(zip(sources, staged))
    ]
    for copy in copies:
        copy.start()
    for extra, extra_out in zip(extras, extra_outs):
        extra_out[...] = extra[...]
    slot = 0
    for copy, stage, heads in zip(copies, staged, per_owner):
        copy.wait()
        tokens, total, width = stage.shape
        wide[...] = stage[...].astype(F32).reshape(tokens * total, width)
        for head in range(total):
            out_ref[head // heads, slot + head % heads] = wide[
                pl.ds(head, tokens, stride=total), :
            ].astype(BF16)
        slot += heads


def pack(owners, sources, *extras):
    tokens, total, width = sources[0].shape
    per_owner = [source.shape[1] // owners for source in sources]
    size = sum(source.size for source in sources)
    return pl.pallas_call(
        functools.partial(pack_body, per_owner, len(extras)),
        out_shape=[
            jax.ShapeDtypeStruct((owners, sum(per_owner), tokens, width), BF16),
        ] + [jax.ShapeDtypeStruct(extra.shape, extra.dtype) for extra in extras],
        in_specs=[pl.BlockSpec(memory_space=pltpu.HBM)] * len(sources) + [VMEM] * len(extras),
        out_specs=[VMEM] * (1 + len(extras)),
        scratch_shapes=[pltpu.VMEM(source.shape, BF16) for source in sources] + [
            pltpu.VMEM((tokens * total, width), F32),
            pltpu.SemaphoreType.DMA((len(sources),)),
        ],
        compiler_params=pltpu.CompilerParams(vmem_limit_bytes=VMEM_BYTES),
        cost_estimate=pl.CostEstimate(flops=size, bytes_accessed=4 * size, transcendentals=0),
    )(*[pltpu.with_memory_space_constraint(source, pltpu.HBM) for source in sources], *extras)


def pack_apart_body(place_ref, key_ref, value_ref, *refs):
    outs, staged, wide, sems = refs[:-4], refs[-4:-2], refs[-2], refs[-1]
    copies = [
        pltpu.make_async_copy(source, stage, sems.at[index])
        for index, (source, stage) in enumerate(zip((key_ref, value_ref), staged))
    ]
    for copy in copies:
        copy.start()
    owners = len(outs)
    for slot, (copy, stage) in enumerate(zip(copies, staged)):
        copy.wait()
        tokens, total, width = stage.shape
        wide[...] = stage[...].astype(F32).reshape(tokens * total, width)
        for step, out_ref in enumerate(outs):
            head = (place_ref[0] + step) % owners
            out_ref[slot] = wide[pl.ds(head, tokens, stride=total), :].astype(BF16)


def pack_apart(place, keys, values):
    tokens, heads, width = keys.shape
    return pl.pallas_call(
        pack_apart_body,
        out_shape=[jax.ShapeDtypeStruct((2, tokens, width), BF16)] * heads,
        in_specs=[SMEM, HBM, HBM],
        out_specs=[VMEM] * heads,
        scratch_shapes=[pltpu.VMEM(keys.shape, BF16)] * 2 + [
            pltpu.VMEM((tokens * heads, width), F32),
            pltpu.SemaphoreType.DMA((2,)),
        ],
        compiler_params=pltpu.CompilerParams(vmem_limit_bytes=VMEM_BYTES),
        cost_estimate=pl.CostEstimate(
            flops=2 * keys.size, bytes_accessed=8 * keys.size, transcendentals=0
        ),
    )(
        place,
        pltpu.with_memory_space_constraint(keys, pltpu.HBM),
        pltpu.with_memory_space_constraint(values, pltpu.HBM),
    )


def gather_pieces_body(place_ref, *refs):
    pieces, out_ref = refs[:-1], refs[-1]
    owners = len(pieces)
    for step, piece in zip((0,) + STEP_ORDER, pieces):
        out_ref[(place_ref[0] + owners - step) % owners] = piece[...]


def gather_pieces(place, pieces):
    shape = (len(pieces),) + pieces[0].shape
    size = len(pieces) * pieces[0].size
    return pl.pallas_call(
        gather_pieces_body,
        out_shape=jax.ShapeDtypeStruct(shape, BF16),
        in_specs=[SMEM] + [VMEM] * len(pieces),
        out_specs=VMEM,
        compiler_params=pltpu.CompilerParams(vmem_limit_bytes=VMEM_BYTES),
        cost_estimate=pl.CostEstimate(flops=size, bytes_accessed=4 * size, transcendentals=0),
    )(place, *pieces)


def unpack_queries_body(in_ref, out_ref, wide):
    owners = in_ref.shape[0]
    tokens, total, width = out_ref.shape
    heads = total // owners
    for head in range(total):
        first = (head % heads) * tokens
        wide[pl.ds(head, tokens, stride=total), :] = (
            in_ref[head // heads, first:first + tokens, :].astype(F32)
        )
    out_ref[...] = wide[...].reshape(tokens, total, width).astype(BF16)


def unpack_queries(received, tokens):
    owners, rows, width = received.shape
    heads = owners * (rows // tokens)
    return call(
        unpack_queries_body,
        jax.ShapeDtypeStruct((tokens, heads, width), BF16),
        [pltpu.VMEM((tokens * heads, width), F32)],
        received.size, 4 * received.size, 0, received,
    )


def unpack_gains_body(in_ref, gain_ref):
    owners, rows, _ = in_ref.shape
    pieces = in_ref[0, rows - TAIL_ROWS:, :].astype(F32)
    for owner in range(1, owners):
        pieces = pieces + in_ref[owner, rows - TAIL_ROWS:, :].astype(F32)
    for row in range(2):
        gain_ref[row:row + 1, :] = jnp.sum(pieces[3 * row:3 * row + 3], axis=0, keepdims=True)


def unpack_gains(received):
    width = received.shape[-1]
    return call(
        unpack_gains_body,
        jax.ShapeDtypeStruct((2, width), F32),
        [], 64 * width, 64 * width, 0, received,
    )


def unpack_keys_body(in_ref, key_out, value_out, wide):
    tokens, owners, width = key_out.shape
    for slot, out_ref in enumerate((key_out, value_out)):
        for head in range(owners):
            wide[slot, pl.ds(head, tokens, stride=owners), :] = in_ref[head, slot].astype(F32)
        out_ref[...] = wide[slot].reshape(tokens, owners, width).astype(BF16)


def unpack_keys(received):
    owners, _, tokens, width = received.shape
    shape = (tokens, owners, width)
    return call(
        unpack_keys_body,
        [jax.ShapeDtypeStruct(shape, BF16)] * 2,
        [pltpu.VMEM((2, tokens * owners, width), F32)],
        received.size, 4 * received.size, 0, received,
    )


def unit_and_inverse(raw):
    widened = raw.astype(F32)
    inverse = lax.rsqrt(jnp.mean(widened * widened, axis=-1, keepdims=True) + epsilon)
    return widened * inverse, inverse


def normalize_back(normed_grad, unit_rows, inverse, gain_values):
    scaled = normed_grad * gain_values
    return inverse * (scaled - unit_rows * jnp.mean(scaled * unit_rows, axis=-1, keepdims=True))


def contract_last(left, right):
    return lax.dot_general(left, right, (((1,), (1,)), ((), ())), preferred_element_type=F32)


def matmul(left, right):
    return lax.dot_general(left, right, (((1,), (0,)), ((), ())), preferred_element_type=F32)


def fold_rows(tile, combine):
    return combine(tile.reshape(tile.shape[0] // 8, 8, tile.shape[1]), axis=0)


def three_pieces(value):
    high = value.astype(BF16)
    rest = value - high.astype(F32)
    middle = rest.astype(BF16)
    return [high, middle, (rest - middle.astype(F32)).astype(BF16)]


def attend_body(
    qd_ref, own_ref, prev_ref, doc_ref, both_gains_ref,
    qgrad_ref, dk_own_ref, dv_own_ref, back_ref,
    key_rows, value_rows, key_cols, value_cols, key_docs,
    score_buf, power_buf, grad_buf, dk_acc, dv_acc, gain_acc, back_buf, back_sem,
):
    blocks, _, rows, width = qd_ref.shape
    tiles = blocks + 1
    window = tiles * rows
    query_gain = both_gains_ref[0:1, :]
    key_gain = both_gains_ref[1:2, :]
    for block in range(2 * blocks):
        source = prev_ref if block < blocks else own_ref
        span = slice(block * rows, (block + 1) * rows)
        unit, _ = unit_and_inverse(source[block % blocks, 0])
        normed = (unit * key_gain).astype(BF16)
        values = source[block % blocks, 1]
        key_rows[span, :] = normed
        value_rows[span, :] = values
        key_cols[:, span] = normed.T
        value_cols[:, span] = values.T
        key_docs[span, :] = jnp.broadcast_to(doc_ref[:, span], (rows, rows)).T
    gain_acc[...] = jnp.zeros_like(gain_acc)

    back_copy = pltpu.make_async_copy(back_buf, back_ref, back_sem)
    key_index = lax.broadcasted_iota(jnp.int32, (rows, rows), 0)
    query_index = lax.broadcasted_iota(jnp.int32, (rows, rows), 1)
    CHUNK = 1

    def accumulate(total, block, terms):
        first, last = block * rows, block * rows + window
        seen = last - rows if block else first
        if block:
            total[first:seen, :] += terms[:seen - first]
        total[seen:last, :] = terms[seen - first:]

    def finish_part(source, index, place):
        unit, _ = unit_and_inverse(source[index, 0])
        part = dk_acc[place * rows:(place + 1) * rows, :] * score_scale
        gain_acc[8:16, :] += fold_rows(part * unit, jnp.sum)
        return part

    def powers_of(block, ready):
        slot = block % 2
        query_unit, query_inverse = unit_and_inverse(qd_ref[block, 0:2].reshape(2 * rows, width))
        query = (query_unit * query_gain).astype(BF16)
        query_docs = doc_ref[:, (block + blocks) * rows:(block + blocks + 1) * rows]
        peak = jnp.full((8, 2 * rows), masked_score, F32)
        for first in range(0, tiles, CHUNK):
            lead = (block + first) * rows
            raw = contract_last(key_rows[lead:lead + CHUNK * rows, :], query)
            for tile in range(first, first + CHUNK):
                span = slice((block + tile) * rows, (block + tile + 1) * rows)
                allowed = key_docs[span, :] == query_docs
                if tile == 0:
                    allowed = allowed & (key_index > query_index)
                if tile == tiles - 1:
                    allowed = allowed & (key_index <= query_index)
                scores = raw[(tile - first) * rows:(tile - first + 1) * rows]
                scores = jnp.concatenate(
                    [
                        jnp.where(allowed, scores[:, :rows], masked_score),
                        jnp.where(allowed, scores[:, rows:], masked_score),
                    ],
                    axis=1,
                )
                score_buf[slot, tile * rows:(tile + 1) * rows, :] = scores
                peak = jnp.maximum(peak, fold_rows(scores, jnp.max))
            yield
        peak = jnp.max(peak, axis=0, keepdims=True) * exponent_scale
        total = jnp.zeros((8, 2 * rows), F32)
        for tile in range(tiles):
            local = slice(tile * rows, (tile + 1) * rows)
            powers = jnp.exp2(score_buf[slot, local, :] * exponent_scale - peak)
            power_buf[slot, local, :] = powers.astype(BF16)
            total = total + fold_rows(powers, jnp.sum)
            yield
        ready[block] = (
            query_unit, query_inverse, query, 1.0 / jnp.sum(total, axis=0, keepdims=True)
        )

    def gradients_of(block, query_unit, query_inverse, query, inverse_total):
        slot = block % 2
        reach = slice(block * rows, block * rows + window)
        out_grad = qd_ref[block, 2:4].reshape(2 * rows, width)
        out_cols = matmul(value_cols[:, reach], power_buf[slot]) * inverse_total
        out_grad_cols = jnp.concatenate(
            [out_grad[:rows].T, out_grad[rows:].T], axis=1
        ).astype(F32) * inverse_total
        scaled_cols = out_grad_cols.astype(BF16)
        yield
        row_dots = jnp.sum(
            scaled_cols.astype(F32) * out_cols.astype(BF16).astype(F32), axis=0, keepdims=True
        )
        scaled_rows = jnp.concatenate([scaled_cols[:, :rows].T, scaled_cols[:, rows:].T], axis=0)
        for first in range(0, tiles, CHUNK):
            local = slice(first * rows, (first + CHUNK) * rows)
            span = slice((block + first) * rows, (block + first + CHUNK) * rows)
            prob_grad = matmul(value_rows[span, :], scaled_cols)
            grad_buf[slot, local, :] = (
                power_buf[slot, local, :].astype(F32) * (prob_grad - row_dots)
            ).astype(BF16)
            yield
        accumulate(dv_acc, block, matmul(power_buf[slot], scaled_rows))
        yield
        accumulate(dk_acc, block, matmul(grad_buf[slot], query))
        yield
        key_part = finish_part(prev_ref, block, block)
        back_buf[block, 0] = key_part.astype(BF16)
        back_buf[block, 1] = dv_acc[block * rows:(block + 1) * rows, :].astype(BF16)
        yield
        query_cols = matmul(key_cols[:, reach], grad_buf[slot])
        yield
        normed_grad = (
            jnp.concatenate([query_cols[:, :rows].T, query_cols[:, rows:].T], axis=0) * score_scale
        )
        gain_acc[0:8, :] += fold_rows(normed_grad * query_unit, jnp.sum)
        query_grad = normalize_back(normed_grad, query_unit, query_inverse, query_gain)
        qgrad_ref[block, 0:2 * rows, :] = query_grad.astype(BF16)

    ready = {}
    for _ in powers_of(0, ready):
        pass
    for block in range(blocks):
        streams = [gradients_of(block, *ready[block])]
        if block + 1 < blocks:
            streams.append(powers_of(block + 1, ready))
        while streams:
            streams = [stream for stream in streams if next(stream, stream) is not stream]

    back_copy.start()
    for block in range(blocks):
        dk_own_ref[block] = finish_part(own_ref, block, block + blocks)
        dv_own_ref[block] = dv_acc[(block + blocks) * rows:(block + blocks + 1) * rows, :]
    tail = []
    for first in (0, 8):
        tail += three_pieces(jnp.sum(gain_acc[first:first + 8, :], axis=0, keepdims=True))
    tail = jnp.concatenate(
        [piece.astype(F32) for piece in tail] + [jnp.zeros((10, width), F32)], axis=0
    ).astype(BF16)
    for block in range(blocks):
        qgrad_ref[block, 2 * rows:, :] = tail
    back_copy.wait()


def attend(queries, own, prev, docs, gains):
    blocks, _, rows, width = own.shape
    window = (blocks + 1) * rows
    tile_flops = 2 * window * 2 * rows * width
    return call(
        attend_body,
        [
            jax.ShapeDtypeStruct((blocks, 2 * rows + TAIL_ROWS, width), BF16),
            jax.ShapeDtypeStruct((blocks, rows, width), F32),
            jax.ShapeDtypeStruct((blocks, rows, width), F32),
            pltpu.HBM((blocks, 2, rows, width), BF16),
        ],
        [
            pltpu.VMEM((2 * blocks * rows, width), BF16),
            pltpu.VMEM((2 * blocks * rows, width), BF16),
            pltpu.VMEM((width, 2 * blocks * rows), BF16),
            pltpu.VMEM((width, 2 * blocks * rows), BF16),
            pltpu.VMEM((2 * blocks * rows, rows), jnp.int32),
            pltpu.VMEM((2, window, 2 * rows), F32),
            pltpu.VMEM((2, window, 2 * rows), BF16),
            pltpu.VMEM((2, window, 2 * rows), BF16),
            pltpu.VMEM((2 * blocks * rows, width), F32),
            pltpu.VMEM((2 * blocks * rows, width), F32),
            pltpu.VMEM((16, width), F32),
            pltpu.VMEM((blocks, 2, rows, width), BF16),
            pltpu.SemaphoreType.DMA,
        ],
        6 * blocks * tile_flops,
        32 * own.size,
        blocks * window * 2 * rows,
        queries, own, prev, docs, gains,
        vmem_bytes=20 << 20,
    )


def finish_keys_body(own_ref, dk_ref, dv_ref, back_ref, gains_ref, out_ref):
    key_gain = gains_ref[1:2, :]
    for block in range(own_ref.shape[0]):
        unit, inverse = unit_and_inverse(own_ref[block, 0])
        key_total = dk_ref[block] + back_ref[block, 0].astype(F32)
        value_total = dv_ref[block] + back_ref[block, 1].astype(F32)
        out_ref[block, 0] = normalize_back(key_total, unit, inverse, key_gain).astype(BF16)
        out_ref[block, 1] = value_total.astype(BF16)


def finish_keys(own, dk_own, dv_own, back, gains):
    return call(
        finish_keys_body,
        jax.ShapeDtypeStruct(own.shape, BF16),
        [], 10 * own.size, 8 * own.size, 0,
        own, dk_own, dv_own, back, gains,
    )


def shifted_terms(value, axis):
    count = lax.axis_size(axis)
    return [
        lax.ppermute(value, axis, [(i, (i + step) % count) for i in range(count)])
        for step in range(1, count)
    ]


def add_terms(value, terms):
    for term in terms:
        value = value + term
    return value


def shifted_sum(value, axis):
    return add_terms(value, shifted_terms(value, axis))


def per_device(ring_axes, query_raw, key_raw, value_matrix, query_gain, key_gain, doc_ids, output_gradient):
    ring_size = lax.axis_size("z")
    rings = lax.axis_size(ring_axes)
    rows = query_raw.shape[0]
    span = ring_size * rows
    forward = [(ring, ring + 1) for ring in range(rings - 1)]
    backward = [(ring + 1, ring) for ring in range(rings - 1)]

    def exchange(value):
        return lax.all_to_all(value, "z", 0, 0, tiled=True)

    def exchange_apart(pieces):
        got = list(pieces)
        for step in STEP_ORDER:
            got[step] = lax.ppermute(
                pieces[step], "z", [(i, (i + step) % ring_size) for i in range(ring_size)]
            )
        return got

    doc_padded = jnp.concatenate([jnp.full((span,), -1, jnp.int32), doc_ids])
    docs = lax.dynamic_slice_in_dim(
        doc_padded, lax.axis_index(ring_axes) * span, 2 * span, 0
    ).reshape(1, 2 * span)
    place = lax.axis_index("z").astype(jnp.int32).reshape(1)
    pieces = pack_apart(place, key_raw, value_matrix)
    pieces = exchange_apart(pieces)
    sent_queries, gains = pack(
        ring_size, (query_raw, output_gradient), jnp.stack([query_gain, key_gain])
    )
    pieces = [pieces[step] for step in (0,) + STEP_ORDER]
    pieces, sent_queries = lax.optimization_barrier((pieces, sent_queries))
    own = gather_pieces(place, pieces)
    prev = lax.ppermute(own, ring_axes, forward)
    queries = exchange(sent_queries)
    query_back, dk_own, dv_own, back = attend(queries, own, prev, docs, gains)
    got_back = lax.ppermute(back, ring_axes, backward)
    got_queries = exchange(query_back)
    query_grad = unpack_queries(got_queries, rows)
    gain_sum = shifted_sum(unpack_gains(got_queries), "kv")
    got_back, gain_sum = lax.optimization_barrier((got_back, gain_sum))
    got_keys = exchange(finish_keys(own, dk_own, dv_own, got_back, gains))
    gain_sum = shifted_sum(gain_sum, "y")
    key_grad, value_grad = unpack_keys(got_keys)
    terms = shifted_terms(gain_sum, "x")
    key_grad, terms = lax.optimization_barrier((key_grad, terms))
    gain_sum = add_terms(gain_sum, terms) / doc_ids.shape[0]
    return query_grad, key_grad, value_grad, gain_sum[0], gain_sum[1]


def solution(mesh):
    ring_size = LOOKBACK_SPAN // 128
    grid = Mesh(mesh.devices.reshape(4, 4, ring_size, 2), ("x", "y", "z", "kv"))
    split = P(("x", "y", "z"), "kv", None)
    return jax.shard_map(
        functools.partial(per_device, ("x", "y")),
        mesh=grid,
        in_specs=(split, split, split, P(), P(), P(), split),
        out_specs=(split, split, split, P(), P()),
        check_vma=False,
    )
```

```python
import functools
import jax
import jax.numpy as jnp
from jax import lax
from jax.experimental import pallas as pl
from jax.experimental.pallas import tpu as pltpu
from jax.sharding import Mesh, PartitionSpec as P

LOOKBACK_SPAN = 1024
epsilon = 1e-06
score_scale = 168.0 ** (-0.5)
exponent_scale = score_scale * 1.4426950408889634
masked_score = -1e30
F32 = jnp.float32
BF16 = jnp.bfloat16
TAIL_ROWS = 16
STEP_ORDER = (1, 7, 2, 6, 4, 3, 5)
VMEM_BYTES = 8 << 20
SMEM = pl.BlockSpec(memory_space=pltpu.SMEM)
HBM = pl.BlockSpec(memory_space=pltpu.HBM)
VMEM = pl.BlockSpec(memory_space=pltpu.VMEM)


def call(body, out_shape, scratch, flops, moved, exps, *args, vmem_bytes=VMEM_BYTES):
    return pl.pallas_call(
        body,
        out_shape=out_shape,
        in_specs=[VMEM] * len(args),
        out_specs=jax.tree.map(
            lambda out: HBM if getattr(out, "memory_space", None) == pltpu.HBM else VMEM,
            out_shape,
        ),
        scratch_shapes=scratch,
        compiler_params=pltpu.CompilerParams(vmem_limit_bytes=vmem_bytes),
        cost_estimate=pl.CostEstimate(flops=flops, bytes_accessed=moved, transcendentals=exps),
    )(*args)


def pack_body(per_owner, passed, *refs):
    count = len(per_owner)
    sources, extras, refs = refs[:count], refs[count:count + passed], refs[count + passed:]
    out_ref, extra_outs = refs[0], refs[1:1 + passed]
    staged, wide, sems = refs[1 + passed:-2], refs[-2], refs[-1]
    copies = [
        pltpu.make_async_copy(source, stage, sems.at[index])
        for index, (source, stage) in enumerate(zip(sources, staged))
    ]
    for copy in copies:
        copy.start()
    for extra, extra_out in zip(extras, extra_outs):
        extra_out[...] = extra[...]
    slot = 0
    for copy, stage, heads in zip(copies, staged, per_owner):
        copy.wait()
        tokens, total, width = stage.shape
        wide[...] = stage[...].astype(F32).reshape(tokens * total, width)
        for head in range(total):
            out_ref[head // heads, slot + head % heads] = wide[
                pl.ds(head, tokens, stride=total), :
            ].astype(BF16)
        slot += heads


def pack(owners, sources, *extras):
    tokens, total, width = sources[0].shape
    per_owner = [source.shape[1] // owners for source in sources]
    size = sum(source.size for source in sources)
    return pl.pallas_call(
        functools.partial(pack_body, per_owner, len(extras)),
        out_shape=[
            jax.ShapeDtypeStruct((owners, sum(per_owner), tokens, width), BF16),
        ] + [jax.ShapeDtypeStruct(extra.shape, extra.dtype) for extra in extras],
        in_specs=[pl.BlockSpec(memory_space=pltpu.HBM)] * len(sources) + [VMEM] * len(extras),
        out_specs=[VMEM] * (1 + len(extras)),
        scratch_shapes=[pltpu.VMEM(source.shape, BF16) for source in sources] + [
            pltpu.VMEM((tokens * total, width), F32),
            pltpu.SemaphoreType.DMA((len(sources),)),
        ],
        compiler_params=pltpu.CompilerParams(vmem_limit_bytes=VMEM_BYTES),
        cost_estimate=pl.CostEstimate(flops=size, bytes_accessed=4 * size, transcendentals=0),
    )(*[pltpu.with_memory_space_constraint(source, pltpu.HBM) for source in sources], *extras)


def pack_apart_body(place_ref, key_ref, value_ref, *refs):
    outs, staged, wide, sems = refs[:-4], refs[-4:-2], refs[-2], refs[-1]
    copies = [
        pltpu.make_async_copy(source, stage, sems.at[index])
        for index, (source, stage) in enumerate(zip((key_ref, value_ref), staged))
    ]
    for copy in copies:
        copy.start()
    owners = len(outs)
    for slot, (copy, stage) in enumerate(zip(copies, staged)):
        copy.wait()
        tokens, total, width = stage.shape
        wide[...] = stage[...].astype(F32).reshape(tokens * total, width)
        for step, out_ref in enumerate(outs):
            head = (place_ref[0] + step) % owners
            out_ref[slot] = wide[pl.ds(head, tokens, stride=total), :].astype(BF16)


def pack_apart(place, keys, values):
    tokens, heads, width = keys.shape
    return pl.pallas_call(
        pack_apart_body,
        out_shape=[jax.ShapeDtypeStruct((2, tokens, width), BF16)] * heads,
        in_specs=[SMEM, HBM, HBM],
        out_specs=[VMEM] * heads,
        scratch_shapes=[pltpu.VMEM(keys.shape, BF16)] * 2 + [
            pltpu.VMEM((tokens * heads, width), F32),
            pltpu.SemaphoreType.DMA((2,)),
        ],
        compiler_params=pltpu.CompilerParams(vmem_limit_bytes=VMEM_BYTES),
        cost_estimate=pl.CostEstimate(
            flops=2 * keys.size, bytes_accessed=8 * keys.size, transcendentals=0
        ),
    )(
        place,
        pltpu.with_memory_space_constraint(keys, pltpu.HBM),
        pltpu.with_memory_space_constraint(values, pltpu.HBM),
    )


def gather_pieces_body(place_ref, *refs):
    pieces, out_ref = refs[:-1], refs[-1]
    owners = len(pieces)
    for step, piece in zip((0,) + STEP_ORDER, pieces):
        out_ref[(place_ref[0] + owners - step) % owners] = piece[...]


def gather_pieces(place, pieces):
    shape = (len(pieces),) + pieces[0].shape
    size = len(pieces) * pieces[0].size
    return pl.pallas_call(
        gather_pieces_body,
        out_shape=jax.ShapeDtypeStruct(shape, BF16),
        in_specs=[SMEM] + [VMEM] * len(pieces),
        out_specs=VMEM,
        compiler_params=pltpu.CompilerParams(vmem_limit_bytes=VMEM_BYTES),
        cost_estimate=pl.CostEstimate(flops=size, bytes_accessed=4 * size, transcendentals=0),
    )(place, *pieces)


def unpack_queries_body(in_ref, out_ref, wide):
    owners = in_ref.shape[0]
    tokens, total, width = out_ref.shape
    heads = total // owners
    for head in range(total):
        first = (head % heads) * tokens
        wide[pl.ds(head, tokens, stride=total), :] = (
            in_ref[head // heads, first:first + tokens, :].astype(F32)
        )
    out_ref[...] = wide[...].reshape(tokens, total, width).astype(BF16)


def unpack_queries(received, tokens):
    owners, rows, width = received.shape
    heads = owners * (rows // tokens)
    return call(
        unpack_queries_body,
        jax.ShapeDtypeStruct((tokens, heads, width), BF16),
        [pltpu.VMEM((tokens * heads, width), F32)],
        received.size, 4 * received.size, 0, received,
    )


def unpack_gains_body(in_ref, gain_ref):
    owners, rows, _ = in_ref.shape
    pieces = in_ref[0, rows - TAIL_ROWS:, :].astype(F32)
    for owner in range(1, owners):
        pieces = pieces + in_ref[owner, rows - TAIL_ROWS:, :].astype(F32)
    for row in range(2):
        gain_ref[row:row + 1, :] = jnp.sum(pieces[3 * row:3 * row + 3], axis=0, keepdims=True)


def unpack_gains(received):
    width = received.shape[-1]
    return call(
        unpack_gains_body,
        jax.ShapeDtypeStruct((2, width), F32),
        [], 64 * width, 64 * width, 0, received,
    )


def unpack_keys_body(in_ref, key_out, value_out, wide):
    tokens, owners, width = key_out.shape
    for slot, out_ref in enumerate((key_out, value_out)):
        for head in range(owners):
            wide[slot, pl.ds(head, tokens, stride=owners), :] = in_ref[head, slot].astype(F32)
        out_ref[...] = wide[slot].reshape(tokens, owners, width).astype(BF16)


def unpack_keys(received):
    owners, _, tokens, width = received.shape
    shape = (tokens, owners, width)
    return call(
        unpack_keys_body,
        [jax.ShapeDtypeStruct(shape, BF16)] * 2,
        [pltpu.VMEM((2, tokens * owners, width), F32)],
        received.size, 4 * received.size, 0, received,
    )


def unit_and_inverse(raw):
    widened = raw.astype(F32)
    inverse = lax.rsqrt(jnp.mean(widened * widened, axis=-1, keepdims=True) + epsilon)
    return widened * inverse, inverse


def normalize_back(normed_grad, unit_rows, inverse, gain_values):
    scaled = normed_grad * gain_values
    return inverse * (scaled - unit_rows * jnp.mean(scaled * unit_rows, axis=-1, keepdims=True))


def contract_last(left, right):
    return lax.dot_general(left, right, (((1,), (1,)), ((), ())), preferred_element_type=F32)


def matmul(left, right):
    return lax.dot_general(left, right, (((1,), (0,)), ((), ())), preferred_element_type=F32)


def fold_rows(tile, combine):
    return combine(tile.reshape(tile.shape[0] // 8, 8, tile.shape[1]), axis=0)


def three_pieces(value):
    high = value.astype(BF16)
    rest = value - high.astype(F32)
    middle = rest.astype(BF16)
    return [high, middle, (rest - middle.astype(F32)).astype(BF16)]


def attend_body(
    qd_ref, own_ref, prev_ref, doc_ref, both_gains_ref,
    qgrad_ref, dk_own_ref, dv_own_ref, back_ref,
    key_rows, value_rows, key_cols, value_cols, key_docs,
    score_buf, power_buf, grad_buf, dk_acc, dv_acc, gain_acc, back_buf, back_sem,
):
    blocks, _, rows, width = qd_ref.shape
    tiles = blocks + 1
    window = tiles * rows
    query_gain = both_gains_ref[0:1, :]
    key_gain = both_gains_ref[1:2, :]
    for block in range(2 * blocks):
        source = prev_ref if block < blocks else own_ref
        span = slice(block * rows, (block + 1) * rows)
        unit, _ = unit_and_inverse(source[block % blocks, 0])
        normed = (unit * key_gain).astype(BF16)
        values = source[block % blocks, 1]
        key_rows[span, :] = normed
        value_rows[span, :] = values
        key_cols[:, span] = normed.T
        value_cols[:, span] = values.T
        key_docs[span, :] = jnp.broadcast_to(doc_ref[:, span], (rows, rows)).T
    gain_acc[...] = jnp.zeros_like(gain_acc)

    back_copy = pltpu.make_async_copy(back_buf, back_ref, back_sem)
    key_index = lax.broadcasted_iota(jnp.int32, (rows, rows), 0)
    query_index = lax.broadcasted_iota(jnp.int32, (rows, rows), 1)
    CHUNK = 1

    def accumulate(total, block, terms):
        first, last = block * rows, block * rows + window
        seen = last - rows if block else first
        if block:
            total[first:seen, :] += terms[:seen - first]
        total[seen:last, :] = terms[seen - first:]

    def finish_part(source, index, place):
        unit, _ = unit_and_inverse(source[index, 0])
        part = dk_acc[place * rows:(place + 1) * rows, :] * score_scale
        gain_acc[8:16, :] += fold_rows(part * unit, jnp.sum)
        return part

    def powers_of(block, ready):
        slot = block % 2
        query_unit, query_inverse = unit_and_inverse(qd_ref[block, 0:2].reshape(2 * rows, width))
        query = (query_unit * query_gain).astype(BF16)
        query_docs = doc_ref[:, (block + blocks) * rows:(block + blocks + 1) * rows]
        peak = jnp.full((8, 2 * rows), masked_score, F32)
        for first in range(0, tiles, CHUNK):
            lead = (block + first) * rows
            raw = contract_last(key_rows[lead:lead + CHUNK * rows, :], query)
            for tile in range(first, first + CHUNK):
                span = slice((block + tile) * rows, (block + tile + 1) * rows)
                allowed = key_docs[span, :] == query_docs
                if tile == 0:
                    allowed = allowed & (key_index > query_index)
                if tile == tiles - 1:
                    allowed = allowed & (key_index <= query_index)
                scores = raw[(tile - first) * rows:(tile - first + 1) * rows]
                scores = jnp.concatenate(
                    [
                        jnp.where(allowed, scores[:, :rows], masked_score),
                        jnp.where(allowed, scores[:, rows:], masked_score),
                    ],
                    axis=1,
                )
                score_buf[slot, tile * rows:(tile + 1) * rows, :] = scores
                peak = jnp.maximum(peak, fold_rows(scores, jnp.max))
            yield
        peak = jnp.max(peak, axis=0, keepdims=True) * exponent_scale
        total = jnp.zeros((8, 2 * rows), F32)
        for tile in range(tiles):
            local = slice(tile * rows, (tile + 1) * rows)
            powers = jnp.exp2(score_buf[slot, local, :] * exponent_scale - peak)
            power_buf[slot, local, :] = powers.astype(BF16)
            total = total + fold_rows(powers, jnp.sum)
            yield
        ready[block] = (
            query_unit, query_inverse, query, 1.0 / jnp.sum(total, axis=0, keepdims=True)
        )

    def gradients_of(block, query_unit, query_inverse, query, inverse_total):
        slot = block % 2
        reach = slice(block * rows, block * rows + window)
        out_grad = qd_ref[block, 2:4].reshape(2 * rows, width)
        out_cols = matmul(value_cols[:, reach], power_buf[slot]) * inverse_total
        out_grad_cols = jnp.concatenate(
            [out_grad[:rows].T, out_grad[rows:].T], axis=1
        ).astype(F32) * inverse_total
        scaled_cols = out_grad_cols.astype(BF16)
        yield
        row_dots = jnp.sum(
            scaled_cols.astype(F32) * out_cols.astype(BF16).astype(F32), axis=0, keepdims=True
        )
        scaled_rows = jnp.concatenate([scaled_cols[:, :rows].T, scaled_cols[:, rows:].T], axis=0)
        for first in range(0, tiles, CHUNK):
            local = slice(first * rows, (first + CHUNK) * rows)
            span = slice((block + first) * rows, (block + first + CHUNK) * rows)
            prob_grad = matmul(value_rows[span, :], scaled_cols)
            grad_buf[slot, local, :] = (
                power_buf[slot, local, :].astype(F32) * (prob_grad - row_dots)
            ).astype(BF16)
            yield
        accumulate(dv_acc, block, matmul(power_buf[slot], scaled_rows))
        yield
        accumulate(dk_acc, block, matmul(grad_buf[slot], query))
        yield
        key_part = finish_part(prev_ref, block, block)
        back_buf[block, 0] = key_part.astype(BF16)
        back_buf[block, 1] = dv_acc[block * rows:(block + 1) * rows, :].astype(BF16)
        yield
        query_cols = matmul(key_cols[:, reach], grad_buf[slot])
        yield
        normed_grad = (
            jnp.concatenate([query_cols[:, :rows].T, query_cols[:, rows:].T], axis=0) * score_scale
        )
        gain_acc[0:8, :] += fold_rows(normed_grad * query_unit, jnp.sum)
        query_grad = normalize_back(normed_grad, query_unit, query_inverse, query_gain)
        qgrad_ref[block, 0:2 * rows, :] = query_grad.astype(BF16)

    ready = {}
    for _ in powers_of(0, ready):
        pass
    for block in range(blocks):
        streams = [gradients_of(block, *ready[block])]
        if block + 1 < blocks:
            streams.append(powers_of(block + 1, ready))
        while streams:
            streams = [stream for stream in streams if next(stream, stream) is not stream]

    back_copy.start()
    for block in range(blocks):
        dk_own_ref[block] = finish_part(own_ref, block, block + blocks)
        dv_own_ref[block] = dv_acc[(block + blocks) * rows:(block + blocks + 1) * rows, :]
    tail = []
    for first in (0, 8):
        tail += three_pieces(jnp.sum(gain_acc[first:first + 8, :], axis=0, keepdims=True))
    tail = jnp.concatenate(
        [piece.astype(F32) for piece in tail] + [jnp.zeros((10, width), F32)], axis=0
    ).astype(BF16)
    for block in range(blocks):
        qgrad_ref[block, 2 * rows:, :] = tail
    back_copy.wait()


def attend(queries, own, prev, docs, gains):
    blocks, _, rows, width = own.shape
    window = (blocks + 1) * rows
    tile_flops = 2 * window * 2 * rows * width
    return call(
        attend_body,
        [
            jax.ShapeDtypeStruct((blocks, 2 * rows + TAIL_ROWS, width), BF16),
            jax.ShapeDtypeStruct((blocks, rows, width), F32),
            jax.ShapeDtypeStruct((blocks, rows, width), F32),
            pltpu.HBM((blocks, 2, rows, width), BF16),
        ],
        [
            pltpu.VMEM((2 * blocks * rows, width), BF16),
            pltpu.VMEM((2 * blocks * rows, width), BF16),
            pltpu.VMEM((width, 2 * blocks * rows), BF16),
            pltpu.VMEM((width, 2 * blocks * rows), BF16),
            pltpu.VMEM((2 * blocks * rows, rows), jnp.int32),
            pltpu.VMEM((2, window, 2 * rows), F32),
            pltpu.VMEM((2, window, 2 * rows), BF16),
            pltpu.VMEM((2, window, 2 * rows), BF16),
            pltpu.VMEM((2 * blocks * rows, width), F32),
            pltpu.VMEM((2 * blocks * rows, width), F32),
            pltpu.VMEM((16, width), F32),
            pltpu.VMEM((blocks, 2, rows, width), BF16),
            pltpu.SemaphoreType.DMA,
        ],
        6 * blocks * tile_flops,
        32 * own.size,
        blocks * window * 2 * rows,
        queries, own, prev, docs, gains,
        vmem_bytes=20 << 20,
    )


def finish_keys_body(own_ref, dk_ref, dv_ref, back_ref, gains_ref, out_ref):
    key_gain = gains_ref[1:2, :]
    for block in range(own_ref.shape[0]):
        unit, inverse = unit_and_inverse(own_ref[block, 0])
        key_total = dk_ref[block] + back_ref[block, 0].astype(F32)
        value_total = dv_ref[block] + back_ref[block, 1].astype(F32)
        out_ref[block, 0] = normalize_back(key_total, unit, inverse, key_gain).astype(BF16)
        out_ref[block, 1] = value_total.astype(BF16)


def finish_keys(own, dk_own, dv_own, back, gains):
    return call(
        finish_keys_body,
        jax.ShapeDtypeStruct(own.shape, BF16),
        [], 10 * own.size, 8 * own.size, 0,
        own, dk_own, dv_own, back, gains,
    )


def shifted_terms(value, axis):
    count = lax.axis_size(axis)
    return [
        lax.ppermute(value, axis, [(i, (i + step) % count) for i in range(count)])
        for step in range(1, count)
    ]


def add_terms(value, terms):
    for term in terms:
        value = value + term
    return value


def shifted_sum(value, axis):
    return add_terms(value, shifted_terms(value, axis))


def per_device(ring_axes, query_raw, key_raw, value_matrix, query_gain, key_gain, doc_ids, output_gradient):
    ring_size = lax.axis_size("z")
    rings = lax.axis_size(ring_axes)
    rows = query_raw.shape[0]
    span = ring_size * rows
    forward = [(ring, ring + 1) for ring in range(rings - 1)]
    backward = [(ring + 1, ring) for ring in range(rings - 1)]

    def exchange(value):
        return lax.all_to_all(value, "z", 0, 0, tiled=True)

    def exchange_apart(pieces):
        got = list(pieces)
        for step in STEP_ORDER:
            got[step] = lax.ppermute(
                pieces[step], "z", [(i, (i + step) % ring_size) for i in range(ring_size)]
            )
        return got

    doc_padded = jnp.concatenate([jnp.full((span,), -1, jnp.int32), doc_ids])
    docs = lax.dynamic_slice_in_dim(
        doc_padded, lax.axis_index(ring_axes) * span, 2 * span, 0
    ).reshape(1, 2 * span)
    place = lax.axis_index("z").astype(jnp.int32).reshape(1)
    pieces = pack_apart(place, key_raw, value_matrix)
    pieces = exchange_apart(pieces)
    sent_queries, gains = pack(
        ring_size, (query_raw, output_gradient), jnp.stack([query_gain, key_gain])
    )
    pieces = [pieces[step] for step in (0,) + STEP_ORDER]
    pieces, sent_queries = lax.optimization_barrier((pieces, sent_queries))
    own = gather_pieces(place, pieces)
    prev = lax.ppermute(own, ring_axes, forward)
    queries = exchange(sent_queries)
    query_back, dk_own, dv_own, back = attend(queries, own, prev, docs, gains)
    got_back = lax.ppermute(back, ring_axes, backward)
    got_queries = exchange(query_back)
    query_grad = unpack_queries(got_queries, rows)
    gain_sum = shifted_sum(unpack_gains(got_queries), "kv")
    got_back, gain_sum = lax.optimization_barrier((got_back, gain_sum))
    got_keys = exchange(finish_keys(own, dk_own, dv_own, got_back, gains))
    gain_sum = shifted_sum(gain_sum, "y")
    key_grad, value_grad = unpack_keys(got_keys)
    terms = shifted_terms(gain_sum, "x")
    key_grad, terms = lax.optimization_barrier((key_grad, terms))
    gain_sum = add_terms(gain_sum, terms) / doc_ids.shape[0]
    return query_grad, key_grad, value_grad, gain_sum[0], gain_sum[1]


def solution(mesh):
    ring_size = LOOKBACK_SPAN // 128
    grid = Mesh(mesh.devices.reshape(4, 4, ring_size, 2), ("x", "y", "z", "kv"))
    split = P(("x", "y", "z"), "kv", None)
    return jax.shard_map(
        functools.partial(per_device, ("x", "y")),
        mesh=grid,
        in_specs=(split, split, split, P(), P(), P(), split),
        out_specs=(split, split, split, P(), P()),
        check_vma=False,
    )
```
